32 devices in a mesh: grp: 8 (over z, y), mem: 4 (over x, core).
Axes of the slice: x: 2, y: 2, z: 4, core: 2. Of those that a mesh axis runs over, the one named last changes fastest.
Arguments:
- potential: float32 [64, 512, 512], P(('grp', 'mem')), may hold values from -6 to 6
- source: float32 [64, 512, 512], P(('grp', 'mem')), may hold values from -20 to 20
- side_faces: float32 [32, 4, 256], P(('grp', 'mem')), may hold values from -6 to 6
- end_faces: float32 [2, 256, 256], replicated, may hold values from -6 to 6
Outputs:
- corrected: float32 [64, 512, 512], P(('grp', 'mem'))
- correction: float32 [32, 256, 256], P(('grp', 'mem'))
The draws below stay inside these ranges and needn't reach their ends.
All inputs are finite; a program needn't handle non-finite values.
Results may differ from the reference program's by a relative error of at most 0.00002.
Values sent between devices are 32-bit elements; how exact they have to be, the bound alone decides.
No kernel may reach another device: no remote copies, remote signals or barrier semaphores. Data moves between devices by JAX's collectives and lax.ppermute only.
A program may use at most 64 MiB of HBM per device.

```python
import jax
import jax.numpy as jnp
from jax import lax

NF = 512
SWEEPS = 8
NC = 256
NZ = 64
NZC = 32


def draw_source(key, part):
    first_key = jax.random.fold_in(jax.random.fold_in(key, 11), 0)
    values = jax.random.normal(first_key, (NZ, NF, NF), jnp.float32)
    return jnp.clip(values, -20.0, 20.0)


def steps_of(own_key, extent, pieces, least, top_value):
    gain = 1.0
    for axis_at, blocks in pieces:
        steps = jax.random.uniform(jax.random.fold_in(jax.random.fold_in(own_key, 6), axis_at), (blocks,), jnp.float32, least / len(pieces), top_value / len(pieces))
        gain = gain * jnp.repeat(jnp.exp(steps), extent[axis_at] // blocks).reshape((-1,) + (1,) * (len(extent) - 1 - axis_at))
    return gain


def gaussian(rng, shape, scale, most, pieces=(), held_as=jnp.bfloat16):
    array = jax.random.normal(rng, shape, jnp.float32) * scale
    if len(pieces) > 0:
        array = steps_of(rng, shape, pieces, -0.22, 0.18) * array
    return jnp.clip(array, min=-most, max=most).astype(held_as)


def setup_inputs(seed: int = 0) -> dict:
    streams_of = jax.random.split(jax.random.key(seed), 5)
    return {
        "potential": gaussian(streams_of[0], (NZ, NF, NF), 1.0, 6.0, ((0, 32),), jnp.float32),
        "source": draw_source(jax.random.fold_in(streams_of[4], 71), 0),
        "side_faces": gaussian(streams_of[2], (NZC, 4, NC), 1.0, 6.0, ((0, 32),), jnp.float32),
        "end_faces": gaussian(streams_of[3], (2, NC, NC), 1.0, 6.0, (), jnp.float32),
    }


def fine_operator(padded):
    center = padded[1:-1, 1:-1, 1:-1]
    beside = padded[2:, 1:-1, 1:-1] + padded[:-2, 1:-1, 1:-1]
    beside = beside + padded[1:-1, 2:, 1:-1] + padded[1:-1, :-2, 1:-1]
    beside = beside + padded[1:-1, 1:-1, 2:] + padded[1:-1, 1:-1, :-2]
    return 4.0 * (6.0 * center - beside)


def restrict_axis(values, direction, before):
    even_part = lax.slice_in_dim(values, 0, None, 2, direction)
    odd_part = lax.slice_in_dim(values, 1, None, 2, direction)
    length = odd_part.shape[direction]
    earlier = jnp.concatenate([before, lax.slice_in_dim(odd_part, 0, length - 1, 1, direction)], direction)
    return 0.5 * even_part + 0.25 * (odd_part + earlier)


def zero_slice(values, direction):
    return jnp.zeros_like(lax.slice_in_dim(values, 0, 1, 1, direction))


def prolong_axis(values, direction, beyond):
    length = values.shape[direction]
    following = jnp.concatenate([lax.slice_in_dim(values, 1, length, 1, direction), beyond], direction)
    middle = 0.5 * (values + following)
    paired = jnp.stack([values, middle], direction + 1)
    new_shape = list(values.shape)
    new_shape[direction] = 2 * length
    return paired.reshape(new_shape)


def last_slice(values, direction):
    length = values.shape[direction]
    return lax.slice_in_dim(values, length - 1, length, 1, direction)


def side_sum(values, side_faces):
    front_face = side_faces[:, 0:1, :]
    back_face = side_faces[:, 1:2, :]
    left_face = side_faces[:, 2, :][:, :, None]
    right_face = side_faces[:, 3, :][:, :, None]
    front_cells = jnp.concatenate([front_face, values[:, :-1, :]], 1)
    back_cells = jnp.concatenate([values[:, 1:, :], back_face], 1)
    left_cells = jnp.concatenate([left_face, values[:, :, :-1]], 2)
    right_cells = jnp.concatenate([values[:, :, 1:], right_face], 2)
    return (front_cells + back_cells) + (left_cells + right_cells)


def smooth_red_black(forcing, side_faces, end_faces, offset, at_first, at_last, neighbour_fn):
    planes = forcing.shape[0]
    depth_ids = offset + lax.broadcasted_iota(jnp.int32, forcing.shape, 0)
    row_ids = lax.broadcasted_iota(jnp.int32, forcing.shape, 1)
    col_ids = lax.broadcasted_iota(jnp.int32, forcing.shape, 2)
    parity = (depth_ids + row_ids + col_ids) % 2

    def one_sweep(counter, values):
        for colour in (0, 1):
            padded = neighbour_fn(values)
            lower_face = jnp.where(at_first, end_faces[0], padded[0])
            upper_face = jnp.where(at_last, end_faces[1], padded[-1])
            under_plane = jnp.concatenate([lower_face[None], padded[1:planes]], 0)
            over_plane = jnp.concatenate([padded[2:planes + 1], upper_face[None]], 0)
            neighbours = (under_plane + over_plane) + side_sum(values, side_faces)
            values = jnp.where(parity == colour, (forcing + neighbours) / 6.0, values)
        return values

    return lax.fori_loop(0, SWEEPS, one_sweep, jnp.zeros_like(forcing))


def pad_depth(values):
    return jnp.pad(values, ((1, 1), (0, 0), (0, 0)))


def reference(potential, source, side_faces, end_faces):
    residual = source - fine_operator(jnp.pad(potential, 1))
    forcing = residual
    for direction in (0, 1, 2):
        forcing = restrict_axis(forcing, direction, zero_slice(forcing, direction))
    correction = smooth_red_black(forcing, side_faces, end_faces, 0, True, True, pad_depth)
    refined = correction
    for direction in (0, 1, 2):
        refined = prolong_axis(refined, direction, last_slice(refined, direction))
    return potential + refined, correction
```

```python
import functools

import jax
import jax.numpy as jnp
import numpy as np
from jax import lax
from jax.experimental import pallas as pl
from jax.experimental.pallas import tpu as pltpu
from jax.sharding import PartitionSpec as P

SWEEPS = 8
AXES = ("grp", "mem")
PAD = 8
LANES = 128
F32 = jnp.float32
BF16 = jnp.bfloat16
HIGHEST = lax.Precision.HIGHEST
VMEM = pl.BlockSpec(memory_space=pltpu.VMEM)
SMEM = pl.BlockSpec(memory_space=pltpu.SMEM)
ANY = pl.BlockSpec(memory_space=pl.ANY)


def restriction(fine):
    matrix = np.zeros((fine // 2, fine))
    for i in range(fine // 2):
        matrix[i, 2 * i] = 0.5
        matrix[i, 2 * i + 1] = 0.25
        if i > 0:
            matrix[i, 2 * i - 1] = 0.25
    return matrix


def neighbour_sum(n):
    return np.eye(n, k=1) + np.eye(n, k=-1)


def prolongation(coarse):
    matrix = np.zeros((2 * coarse, coarse))
    for i in range(coarse):
        matrix[2 * i, i] = 1.0
        matrix[2 * i + 1, i] += 0.5
        matrix[2 * i + 1, min(i + 1, coarse - 1)] += 0.5
    return matrix


def mode_order(n, devices):
    rows = n // devices
    if rows % 2:
        return np.arange(n)
    half = rows // 2
    low = np.arange(n // 2).reshape(devices, half)
    return np.concatenate([low, n - 1 - low], 1).reshape(-1)


def sine_matrix(n):
    index = np.arange(1, n + 1)
    return np.sqrt(2.0 / (n + 1)) * np.sin(np.pi * np.outer(index, index) / (n + 1))


def split3(x):
    high = x.astype(BF16)
    rest = x - high.astype(F32)
    mid = rest.astype(BF16)
    low = (rest - mid.astype(F32)).astype(BF16)
    return high, mid, low


def dot3(parts_ref, first, weights):
    total = None
    for part in (2, 1, 0):
        term = jnp.dot(parts_ref[first + part], weights, preferred_element_type=F32)
        total = term if total is None else total + term
    return total


def fine_kernel(
    pos_ref, pot_hbm, src_hbm, side_ref, end_hbm, rt_ref, gt_ref,
    own_ref, near_ref, far_ref,
    pot, src, end, mid, parts, sem, end_sem,
):
    fine = pot_hbm.shape[1]
    coarse = fine // 2
    position = pos_ref[0]
    last = pos_ref[1]
    copies = []
    for plane in (0, 1):
        for c in range(fine // LANES):
            for which, (hbm, buf) in enumerate(((pot_hbm, pot), (src_hbm, src))):
                copies.append(
                    pltpu.make_async_copy(
                        hbm.at[plane, :, pl.ds(c * LANES, LANES)],
                        buf.at[plane, c, pl.ds(PAD, fine), :],
                        sem.at[len(copies)],
                    )
                )
                copies[-1].start()
    at_end = jnp.where(position == last, 1, 0)
    end_copy = pltpu.make_async_copy(end_hbm.at[at_end], end, end_sem)
    end_copy.start()
    edge = jnp.zeros((2, fine // LANES, PAD, LANES), F32)
    for buf in (pot, src):
        buf[:, :, 0:PAD, :] = edge
        buf[:, :, PAD + fine : PAD + fine + PAD, :] = edge

    not_first = jnp.where(position > 0, 1.0, 0.0).astype(F32)
    block = 64
    waiting = iter(copies)
    for plane in (0, 1):
        for c in range(fine // LANES):
            next(waiting).wait()
            next(waiting).wait()
            columns = pl.ds(c * LANES, LANES)
            for start in range(0, coarse, block):

                def rows(buf, offset):
                    return buf[plane, c, pl.ds(PAD + 2 * start + offset, block, stride=2), :]

                even = rows(pot, 0)
                odds = rows(pot, 1) + rows(pot, -1)
                a = 0.5 * even + 0.25 * odds
                b = (rows(pot, -2) + rows(pot, 2)) + 2.0 * (odds + even)
                if start == 0:
                    row_ids = lax.broadcasted_iota(jnp.int32, (block, LANES), 0)
                    b = b - jnp.where(row_ids == 0, even, 0.0)
                b = b + (0.5 * rows(src, 0) + 0.25 * (rows(src, 1) + rows(src, -1)))
                where = pl.ds(start, block)
                for part, value in enumerate(split3(a)):
                    parts[3 * plane + part, where, columns] = value
                if plane == 0:
                    mid[where, columns] = a
                    combined = 0.5 * b + not_first * a
                else:
                    combined = 0.25 * b + (2.0 * a + mid[where, columns])
                for part, value in enumerate(split3(combined)):
                    parts[6 + 3 * plane + part, where, columns] = value

    down = dot3(parts, 0, rt_ref[...])
    up = dot3(parts, 9, rt_ref[...]) + 0.25 * dot3(parts, 3, gt_ref[...])
    own = dot3(parts, 6, rt_ref[...]) + 0.5 * dot3(parts, 0, gt_ref[...]) + up

    row_ids = lax.broadcasted_iota(jnp.int32, (coarse, coarse), 0)
    col_ids = lax.broadcasted_iota(jnp.int32, (coarse, coarse), 1)
    side = side_ref[0]
    columns = jnp.transpose(jnp.concatenate([side, side], 0))
    own = own + jnp.where(row_ids == 0, side[0:1], 0.0)
    own = own + jnp.where(row_ids == coarse - 1, side[1:2], 0.0)
    own = own + jnp.where(col_ids == 0, columns[:, 2:3], 0.0)
    own = own + jnp.where(col_ids == coarse - 1, columns[:, 3:4], 0.0)
    end_copy.wait()
    beside_end = jnp.logical_or(position == 0, position == last)
    own_ref[...] = own + jnp.where(beside_end, end[...], 0.0)
    is_even = lax.rem(position, 2) == 0
    near_ref[...] = jnp.where(is_even, up, down)
    far_ref[...] = jnp.where(is_even, down, up)


def fine_stage(position, last, potential, source, side_faces, end_faces):
    fine = potential.shape[1]
    coarse = fine // 2
    r = restriction(fine)
    g = -24.0 * r + 4.0 * (r @ neighbour_sum(fine))
    rt = jnp.asarray(r.T, BF16)
    gt = jnp.asarray(g.T, BF16)
    plane = jax.ShapeDtypeStruct((coarse, coarse), F32)
    return pl.pallas_call(
        fine_kernel,
        out_shape=(plane, plane, plane),
        in_specs=[SMEM, ANY, ANY, VMEM, ANY, VMEM, VMEM],
        out_specs=(VMEM, VMEM, VMEM),
        scratch_shapes=[
            pltpu.VMEM((2, fine // LANES, fine + 2 * PAD, LANES), F32),
            pltpu.VMEM((2, fine // LANES, fine + 2 * PAD, LANES), F32),
            pltpu.VMEM((coarse, coarse), F32),
            pltpu.VMEM((coarse, fine), F32),
            pltpu.VMEM((12, coarse, fine), BF16),
            pltpu.SemaphoreType.DMA((4 * (fine // LANES),)),
            pltpu.SemaphoreType.DMA,
        ],
        name="fine_stage",
    )(jnp.stack([position, last]), potential, source, side_faces, end_faces, rt, gt)


def rows_kernel(own_ref, near_ref, far_ref, sine_ref, out_ref):
    devices, _, rows, coarse = out_ref.shape
    sine = sine_ref[...]
    first = jnp.dot(sine, own_ref[...] + near_ref[...], precision=HIGHEST, preferred_element_type=F32)
    out_ref[:, 0] = first.reshape(devices, rows, coarse)
    second = jnp.dot(sine, far_ref[...], precision=HIGHEST, preferred_element_type=F32)
    out_ref[:, 1] = second.reshape(devices, rows, coarse)


def rows_stage(devices, own, near, far):
    coarse = own.shape[0]
    sine = jnp.asarray(sine_matrix(coarse)[mode_order(coarse, devices)], F32)
    return pl.pallas_call(
        rows_kernel,
        out_shape=jax.ShapeDtypeStruct((devices, 2, coarse // devices, coarse), F32),
        in_specs=[VMEM] * 4,
        out_specs=VMEM,
        name="rows_stage",
    )(own, near, far, sine)


def sweep_kernel(pos_ref, in_ref, alpha_ref, out_ref, values, force):
    planes, _, rows, coarse = in_ref.shape
    paired = rows % 2 == 0
    sixth = 1.0 / 6.0
    shape = (rows, coarse)
    lanes = lax.broadcasted_iota(jnp.int32, shape, 1)
    at_left = lanes == 0
    at_right = lanes == coarse - 1
    alpha = jnp.broadcast_to(alpha_ref[0][:, 0:1], shape)
    for k in range(planes):
        total = in_ref[k, 0]
        if k % 2 == 0 and k > 0:
            total = total + in_ref[k - 1, 1]
        if k % 2 == 1 and k + 1 < planes:
            total = total + in_ref[k + 1, 1]
        total = total * sixth
        force[k] = total
        values[k] = total
    values[planes] = jnp.zeros(shape, F32)

    def applied(k, under, here, over):
        left = jnp.where(at_left, 0.0, pltpu.roll(here, 1, 1))
        right = jnp.where(at_right, 0.0, pltpu.roll(here, coarse - 1, 1))
        return (force[k] + alpha * here) + sixth * ((under + over) + (left + right))

    def step(counter, carry):
        under = jnp.zeros(shape, F32)
        here = values[0]
        for k in range(planes):
            over = values[k + 1]
            values[k] = applied(k, under, here, over)
            under, here = here, over
        return carry

    lax.fori_loop(0, 2 * SWEEPS - 2, step, 0)

    under = jnp.zeros(shape, F32)
    here = values[0]
    for k in range(planes):
        over = values[k + 1]
        black = applied(k, under, here, over)
        mean = 0.5 * (here + black)
        swing = 0.5 * (here - black)
        swing = jnp.where((lanes + k) % 2 == 0, swing, -swing)
        if paired:
            fields = [mean + pltpu.roll(swing, rows // 2, 0)]
        else:
            fields = [mean, swing]
        for f, field in enumerate(fields):
            out_ref[k, 2 * f] = field
            if k > 0:
                out_ref[k - 1, 2 * f + 1] = field
            if k == planes - 1:
                out_ref[k, 2 * f + 1] = field
        under, here = here, over


def sweep_stage(position, received):
    devices, _, rows, coarse = received.shape
    fields = 2 if rows % 2 == 0 else 4
    modes = mode_order(coarse, devices) + 1
    alpha = np.cos(np.pi * modes / (coarse + 1)) / 3.0
    table = jnp.asarray(np.tile(alpha.reshape(devices, rows, 1), (1, 1, 128)), F32)
    return pl.pallas_call(
        sweep_kernel,
        out_shape=jax.ShapeDtypeStruct((devices, fields, rows, coarse), F32),
        grid_spec=pltpu.PrefetchScalarGridSpec(
            num_scalar_prefetch=1,
            grid=(1,),
            in_specs=[
                pl.BlockSpec((devices, 2, rows, coarse), lambda i, pos: (0, 0, 0, 0)),
                pl.BlockSpec((1, rows, 128), lambda i, pos: (pos[0], 0, 0)),
            ],
            out_specs=pl.BlockSpec((devices, fields, rows, coarse), lambda i, pos: (0, 0, 0, 0)),
            scratch_shapes=[
                pltpu.VMEM((devices + 1, rows, coarse), F32),
                pltpu.VMEM((devices, rows, coarse), F32),
            ],
        ),
        name="sweep_stage",
    )(position[None], received, table)


def finish_kernel(in_ref, back_ref, pt_ref, pot_hbm, out_hbm, corr_ref, pot, out, parts, wide, pot_sem, out_sem):
    devices, fields, rows, coarse = in_ref.shape
    fine = 2 * coarse
    loads, stores = [], []
    for f in (0, 1):
        for c in range(fine // LANES):
            lanes = pl.ds(c * LANES, LANES)
            at = f * (fine // LANES) + c
            loads.append(pltpu.make_async_copy(pot_hbm.at[f, :, lanes], pot.at[f, c], pot_sem.at[at]))
            stores.append(pltpu.make_async_copy(out.at[f, c], out_hbm.at[f, :, lanes], out_sem.at[at]))
    for load in loads:
        load.start()

    def plane(which):
        total = jnp.dot(
            back_ref[0], in_ref[:, which].reshape(coarse, coarse),
            precision=HIGHEST, preferred_element_type=F32,
        )
        if fields == 4:
            total = total + jnp.dot(
                back_ref[1], in_ref[:, which + 2].reshape(coarse, coarse),
                precision=HIGHEST, preferred_element_type=F32,
            )
        return total

    block = 64
    own = plane(0)
    corr_ref[0] = own
    for f in (0, 1):
        value = own if f == 0 else 0.5 * (corr_ref[0] + plane(1))
        for part, piece in enumerate(split3(value)):
            parts[part] = piece
        wide[0:coarse, :] = dot3(parts, 0, pt_ref[...])
        wide[coarse : coarse + 1, :] = wide[coarse - 1 : coarse, :]
        for c in range(fine // LANES):
            lanes = pl.ds(c * LANES, LANES)
            at = f * (fine // LANES) + c
            loads[at].wait()
            for start in range(0, coarse, block):
                here = wide[pl.ds(start, block), lanes]
                after = wide[pl.ds(start + 1, block), lanes]
                evens = pl.ds(2 * start, block, stride=2)
                odds = pl.ds(2 * start + 1, block, stride=2)
                out[f, c, evens, :] = pot[f, c, evens, :] + here
                out[f, c, odds, :] = pot[f, c, odds, :] + 0.5 * (here + after)
            stores[at].start()
    for store in stores:
        store.wait()


def finish_stage(potential, received):
    devices, fields, rows, coarse = received.shape
    fine = 2 * coarse
    order = mode_order(coarse, devices)
    sine = sine_matrix(coarse)
    back = [sine[order].T]
    if fields == 4:
        back.append(sine[coarse - 1 - order].T)
    return pl.pallas_call(
        finish_kernel,
        out_shape=(
            jax.ShapeDtypeStruct((2, fine, fine), F32),
            jax.ShapeDtypeStruct((1, coarse, coarse), F32),
        ),
        in_specs=[VMEM, VMEM, VMEM, ANY],
        out_specs=(ANY, VMEM),
        scratch_shapes=[
            pltpu.VMEM((2, fine // LANES, fine, LANES), F32),
            pltpu.VMEM((2, fine // LANES, fine, LANES), F32),
            pltpu.VMEM((3, coarse, coarse), BF16),
            pltpu.VMEM((coarse + PAD, fine), F32),
            pltpu.SemaphoreType.DMA((2 * (fine // LANES),)),
            pltpu.SemaphoreType.DMA((2 * (fine // LANES),)),
        ],
        name="finish_stage",
    )(received, jnp.asarray(np.stack(back), F32), jnp.asarray(prolongation(coarse).T, BF16), potential)


def per_device(potential, source, side_faces, end_faces):
    devices = lax.axis_size("grp") * lax.axis_size("mem")
    position = (lax.axis_index("grp") * lax.axis_size("mem") + lax.axis_index("mem")).astype(jnp.int32)
    last = jnp.int32(devices - 1)
    own, near, far = fine_stage(position, last, potential, source, side_faces, end_faces)
    near = lax.ppermute(near, AXES, [(i, i ^ 1) for i in range(devices)])
    sent = rows_stage(devices, own, near, far)
    received = lax.all_to_all(sent, AXES, 0, 0, tiled=True)
    solved = sweep_stage(position, received)
    returned = lax.all_to_all(solved, AXES, 0, 0, tiled=True)
    return finish_stage(potential, returned)


def solution(mesh):
    split = P(AXES, None, None)
    return jax.shard_map(
        per_device,
        mesh=mesh,
        in_specs=(split, split, split, P()),
        out_specs=(split, split),
        check_vma=False,
    )
```

```python
import jax
import jax.numpy as jnp
import numpy as np
from jax import lax
from jax.experimental import pallas as pl
from jax.experimental.pallas import tpu as pltpu
from jax.sharding import PartitionSpec as P

SWEEPS = 8
AXES = ("grp", "mem")
PAD = 8
LANES = 128
F32 = jnp.float32
BF16 = jnp.bfloat16
HIGHEST = lax.Precision.HIGHEST
VMEM = pl.BlockSpec(memory_space=pltpu.VMEM)
ANY = pl.BlockSpec(memory_space=pl.ANY)
HBM = pl.BlockSpec(memory_space=pltpu.HBM)


def place():
    members = lax.axis_size("mem")
    return lax.axis_index("grp") * members + lax.axis_index("mem"), lax.axis_size("grp") * members


def in_hbm(array):
    return pltpu.with_memory_space_constraint(array, pltpu.HBM)


def room(mebibytes):
    return pltpu.CompilerParams(vmem_limit_bytes=mebibytes << 20)


def restriction(fine):
    matrix = np.zeros((fine // 2, fine))
    for i in range(fine // 2):
        matrix[i, 2 * i] = 0.5
        matrix[i, 2 * i + 1] = 0.25
        if i > 0:
            matrix[i, 2 * i - 1] = 0.25
    return matrix


def neighbour_sum(n):
    return np.eye(n, k=1) + np.eye(n, k=-1)


def prolongation(coarse):
    matrix = np.zeros((2 * coarse, coarse))
    for i in range(coarse):
        matrix[2 * i, i] = 1.0
        matrix[2 * i + 1, i] += 0.5
        matrix[2 * i + 1, min(i + 1, coarse - 1)] += 0.5
    return matrix


def mode_order(n, devices):
    rows = n // devices
    if rows % 2:
        return np.arange(n)
    half = rows // 2
    low = np.arange(n // 2).reshape(devices, half)
    return np.concatenate([low, n - 1 - low], 1).reshape(-1)


def sine_matrix(n):
    index = np.arange(1, n + 1)
    return np.sqrt(2.0 / (n + 1)) * np.sin(np.pi * np.outer(index, index) / (n + 1))


def split3(x):
    high = x.astype(BF16)
    rest = x - high.astype(F32)
    mid = rest.astype(BF16)
    low = (rest - mid.astype(F32)).astype(BF16)
    return high, mid, low


def dot3(parts_ref, first, weights):
    total = None
    for part in (2, 1, 0):
        term = jnp.dot(parts_ref[first + part], weights, preferred_element_type=F32)
        total = term if total is None else total + term
    return total


def fine_kernel(
    pot_hbm, src_hbm, side_hbm, end_hbm, rt_hbm, gt_hbm,
    own_ref, near_ref, far_ref,
    pot, src, side_buf, end, rt_ref, gt_ref, mid, parts, sem, small_sem,
):
    fine = pot_hbm.shape[1]
    coarse = fine // 2
    position, devices = place()
    last = devices - 1
    copies = []
    for plane in (0, 1):
        for c in range(fine // LANES):
            for which, (hbm, buf) in enumerate(((pot_hbm, pot), (src_hbm, src))):
                copies.append(
                    pltpu.make_async_copy(
                        hbm.at[plane, :, pl.ds(c * LANES, LANES)],
                        buf.at[plane, c, pl.ds(PAD, fine), :],
                        sem.at[len(copies)],
                    )
                )
                copies[-1].start()
    at_end = jnp.where(position == last, 1, 0)
    small = [
        pltpu.make_async_copy(rt_hbm, rt_ref, small_sem.at[0]),
        pltpu.make_async_copy(gt_hbm, gt_ref, small_sem.at[1]),
        pltpu.make_async_copy(side_hbm, side_buf, small_sem.at[2]),
        pltpu.make_async_copy(end_hbm.at[at_end], end, small_sem.at[3]),
    ]
    for copy in small:
        copy.start()
    edge = jnp.zeros((2, fine // LANES, PAD, LANES), F32)
    for buf in (pot, src):
        buf[:, :, 0:PAD, :] = edge
        buf[:, :, PAD + fine : PAD + fine + PAD, :] = edge

    not_first = jnp.where(position > 0, 1.0, 0.0).astype(F32)
    block = 64
    waiting = iter(copies)
    for plane in (0, 1):
        for c in range(fine // LANES):
            next(waiting).wait()
            next(waiting).wait()
            columns = pl.ds(c * LANES, LANES)
            for start in range(0, coarse, block):

                def rows(buf, offset):
                    return buf[plane, c, pl.ds(PAD + 2 * start + offset, block, stride=2), :]

                even = rows(pot, 0)
                odds = rows(pot, 1) + rows(pot, -1)
                a = 0.5 * even + 0.25 * odds
                b = (rows(pot, -2) + rows(pot, 2)) + 2.0 * (odds + even)
                if start == 0:
                    row_ids = lax.broadcasted_iota(jnp.int32, (block, LANES), 0)
                    b = b - jnp.where(row_ids == 0, even, 0.0)
                b = b + (0.5 * rows(src, 0) + 0.25 * (rows(src, 1) + rows(src, -1)))
                where = pl.ds(start, block)
                for part, value in enumerate(split3(a)):
                    parts[3 * plane + part, where, columns] = value
                if plane == 0:
                    mid[where, columns] = a
                    combined = 0.5 * b + not_first * a
                else:
                    combined = 0.25 * b + (2.0 * a + mid[where, columns])
                for part, value in enumerate(split3(combined)):
                    parts[6 + 3 * plane + part, where, columns] = value

    for copy in small:
        copy.wait()
    down = dot3(parts, 0, rt_ref[...])
    up = dot3(parts, 9, rt_ref[...]) + 0.25 * dot3(parts, 3, gt_ref[...])
    own = dot3(parts, 6, rt_ref[...]) + 0.5 * dot3(parts, 0, gt_ref[...]) + up

    row_ids = lax.broadcasted_iota(jnp.int32, (coarse, coarse), 0)
    col_ids = lax.broadcasted_iota(jnp.int32, (coarse, coarse), 1)
    side = side_buf[0]
    columns = jnp.transpose(jnp.concatenate([side, side], 0))
    own = own + jnp.where(row_ids == 0, side[0:1], 0.0)
    own = own + jnp.where(row_ids == coarse - 1, side[1:2], 0.0)
    own = own + jnp.where(col_ids == 0, columns[:, 2:3], 0.0)
    own = own + jnp.where(col_ids == coarse - 1, columns[:, 3:4], 0.0)
    beside_end = jnp.logical_or(position == 0, position == last)
    own_ref[...] = own + jnp.where(beside_end, end[...], 0.0)
    is_even = lax.rem(position, 2) == 0
    near_ref[...] = jnp.where(is_even, up, down)
    far_ref[...] = jnp.where(is_even, down, up)


def fine_stage(potential, source, side_faces, end_faces):
    fine = potential.shape[1]
    coarse = fine // 2
    r = restriction(fine)
    g = -24.0 * r + 4.0 * (r @ neighbour_sum(fine))
    rt = jnp.asarray(r.T, BF16)
    gt = jnp.asarray(g.T, BF16)
    plane = jax.ShapeDtypeStruct((coarse, coarse), F32)
    return pl.pallas_call(
        fine_kernel,
        out_shape=(plane, plane, plane),
        in_specs=[HBM] * 6,
        out_specs=(VMEM, VMEM, VMEM),
        scratch_shapes=[
            pltpu.VMEM((2, fine // LANES, fine + 2 * PAD, LANES), F32),
            pltpu.VMEM((2, fine // LANES, fine + 2 * PAD, LANES), F32),
            pltpu.VMEM((1, 4, coarse), F32),
            pltpu.VMEM((coarse, coarse), F32),
            pltpu.VMEM((fine, coarse), BF16),
            pltpu.VMEM((fine, coarse), BF16),
            pltpu.VMEM((coarse, fine), F32),
            pltpu.VMEM((12, coarse, fine), BF16),
            pltpu.SemaphoreType.DMA((4 * (fine // LANES),)),
            pltpu.SemaphoreType.DMA((4,)),
        ],
        compiler_params=room(20),
        name="fine_stage",
    )(in_hbm(potential), in_hbm(source), in_hbm(side_faces), in_hbm(end_faces), in_hbm(rt), in_hbm(gt))


def rows_kernel(own_ref, near_ref, far_ref, sine_ref, out_ref):
    devices, _, rows, coarse = out_ref.shape
    sine = sine_ref[...]
    first = jnp.dot(sine, own_ref[...] + near_ref[...], precision=HIGHEST, preferred_element_type=F32)
    out_ref[:, 0] = first.reshape(devices, rows, coarse)
    second = jnp.dot(sine, far_ref[...], precision=HIGHEST, preferred_element_type=F32)
    out_ref[:, 1] = second.reshape(devices, rows, coarse)


def rows_stage(devices, own, near, far):
    coarse = own.shape[0]
    sine = jnp.asarray(sine_matrix(coarse)[mode_order(coarse, devices)], F32)
    return pl.pallas_call(
        rows_kernel,
        out_shape=jax.ShapeDtypeStruct((devices, 2, coarse // devices, coarse), F32),
        in_specs=[VMEM] * 4,
        out_specs=VMEM,
        compiler_params=room(8),
        name="rows_stage",
    )(own, near, far, sine)


def sweep_kernel(in_ref, alpha_ref, out_ref, values, force):
    planes, _, rows, coarse = in_ref.shape
    paired = rows % 2 == 0
    sixth = 1.0 / 6.0
    shape = (rows, coarse)
    lanes = lax.broadcasted_iota(jnp.int32, shape, 1)
    at_left = lanes == 0
    at_right = lanes == coarse - 1
    alpha = jnp.broadcast_to(alpha_ref[place()[0]][:, 0:1], shape)
    for k in range(planes):
        total = in_ref[k, 0]
        if k % 2 == 0 and k > 0:
            total = total + in_ref[k - 1, 1]
        if k % 2 == 1 and k + 1 < planes:
            total = total + in_ref[k + 1, 1]
        total = total * sixth
        force[k] = total
        values[k] = total
    values[planes] = jnp.zeros(shape, F32)

    def applied(k, under, here, over):
        left = jnp.where(at_left, 0.0, pltpu.roll(here, 1, 1))
        right = jnp.where(at_right, 0.0, pltpu.roll(here, coarse - 1, 1))
        return (force[k] + alpha * here) + sixth * ((under + over) + (left + right))

    def step(counter, carry):
        under = jnp.zeros(shape, F32)
        here = values[0]
        for k in range(planes):
            over = values[k + 1]
            values[k] = applied(k, under, here, over)
            under, here = here, over
        return carry

    lax.fori_loop(0, 2 * SWEEPS - 2, step, 0)

    under = jnp.zeros(shape, F32)
    here = values[0]
    for k in range(planes):
        over = values[k + 1]
        black = applied(k, under, here, over)
        mean = 0.5 * (here + black)
        swing = 0.5 * (here - black)
        swing = jnp.where((lanes + k) % 2 == 0, swing, -swing)
        if paired:
            fields = [mean + pltpu.roll(swing, rows // 2, 0)]
        else:
            fields = [mean, swing]
        for f, field in enumerate(fields):
            out_ref[k, 2 * f] = field
            if k > 0:
                out_ref[k - 1, 2 * f + 1] = field
            if k == planes - 1:
                out_ref[k, 2 * f + 1] = field
        under, here = here, over


def sweep_stage(received):
    devices, _, rows, coarse = received.shape
    fields = 2 if rows % 2 == 0 else 4
    modes = mode_order(coarse, devices) + 1
    alpha = np.cos(np.pi * modes / (coarse + 1)) / 3.0
    table = jnp.asarray(np.tile(alpha.reshape(devices, rows, 1), (1, 1, 128)), F32)
    return pl.pallas_call(
        sweep_kernel,
        out_shape=jax.ShapeDtypeStruct((devices, fields, rows, coarse), F32),
        in_specs=[VMEM, VMEM],
        out_specs=VMEM,
        scratch_shapes=[
            pltpu.VMEM((devices + 1, rows, coarse), F32),
            pltpu.VMEM((devices, rows, coarse), F32),
        ],
        compiler_params=room(8 if rows % 8 == 0 else 24),
        name="sweep_stage",
    )(received, table)


def finish_kernel(in_ref, back_ref, pt_ref, pot_hbm, out_hbm, corr_ref, pot, out, parts, wide, pot_sem, out_sem):
    devices, fields, rows, coarse = in_ref.shape
    fine = 2 * coarse
    loads, stores = [], []
    for f in (0, 1):
        for c in range(fine // LANES):
            lanes = pl.ds(c * LANES, LANES)
            at = f * (fine // LANES) + c
            loads.append(pltpu.make_async_copy(pot_hbm.at[f, :, lanes], pot.at[f, c], pot_sem.at[at]))
            stores.append(pltpu.make_async_copy(out.at[f, c], out_hbm.at[f, :, lanes], out_sem.at[at]))
    for load in loads:
        load.start()

    def plane(which):
        total = jnp.dot(
            back_ref[0], in_ref[:, which].reshape(coarse, coarse),
            precision=HIGHEST, preferred_element_type=F32,
        )
        if fields == 4:
            total = total + jnp.dot(
                back_ref[1], in_ref[:, which + 2].reshape(coarse, coarse),
                precision=HIGHEST, preferred_element_type=F32,
            )
        return total

    block = 64
    own = plane(0)
    corr_ref[0] = own
    for f in (0, 1):
        value = own if f == 0 else 0.5 * (corr_ref[0] + plane(1))
        for part, piece in enumerate(split3(value)):
            parts[part] = piece
        wide[0:coarse, :] = dot3(parts, 0, pt_ref[...])
        wide[coarse : coarse + 1, :] = wide[coarse - 1 : coarse, :]
        for c in range(fine // LANES):
            lanes = pl.ds(c * LANES, LANES)
            at = f * (fine // LANES) + c
            loads[at].wait()
            for start in range(0, coarse, block):
                here = wide[pl.ds(start, block), lanes]
                after = wide[pl.ds(start + 1, block), lanes]
                evens = pl.ds(2 * start, block, stride=2)
                odds = pl.ds(2 * start + 1, block, stride=2)
                out[f, c, evens, :] = pot[f, c, evens, :] + here
                out[f, c, odds, :] = pot[f, c, odds, :] + 0.5 * (here + after)
            stores[at].start()
    for store in stores:
        store.wait()


def finish_stage(potential, received):
    devices, fields, rows, coarse = received.shape
    fine = 2 * coarse
    order = mode_order(coarse, devices)
    sine = sine_matrix(coarse)
    back = [sine[order].T]
    if fields == 4:
        back.append(sine[coarse - 1 - order].T)
    return pl.pallas_call(
        finish_kernel,
        out_shape=(
            jax.ShapeDtypeStruct((2, fine, fine), F32),
            jax.ShapeDtypeStruct((1, coarse, coarse), F32),
        ),
        in_specs=[VMEM, VMEM, VMEM, ANY],
        out_specs=(ANY, VMEM),
        scratch_shapes=[
            pltpu.VMEM((2, fine // LANES, fine, LANES), F32),
            pltpu.VMEM((2, fine // LANES, fine, LANES), F32),
            pltpu.VMEM((3, coarse, coarse), BF16),
            pltpu.VMEM((coarse + PAD, fine), F32),
            pltpu.SemaphoreType.DMA((2 * (fine // LANES),)),
            pltpu.SemaphoreType.DMA((2 * (fine // LANES),)),
        ],
        compiler_params=room(16),
        name="finish_stage",
    )(received, jnp.asarray(np.stack(back), F32), jnp.asarray(prolongation(coarse).T, BF16), potential)


def per_device(potential, source, side_faces, end_faces):
    devices = lax.axis_size("grp") * lax.axis_size("mem")
    own, near, far = fine_stage(potential, source, side_faces, end_faces)
    near = lax.ppermute(near, AXES, [(i, i ^ 1) for i in range(devices)])
    sent = rows_stage(devices, own, near, far)
    received = lax.all_to_all(sent, AXES, 0, 0, tiled=True)
    solved = sweep_stage(received)
    returned = lax.all_to_all(solved, AXES, 0, 0, tiled=True)
    return finish_stage(potential, returned)


def solution(mesh):
    split = P(AXES, None, None)
    return jax.shard_map(
        per_device,
        mesh=mesh,
        in_specs=(split, split, split, P()),
        out_specs=(split, split),
        check_vma=False,
    )
```

```python
import jax
import jax.numpy as jnp
import numpy as np
from jax import lax
from jax.experimental import pallas as pl
from jax.experimental.pallas import tpu as pltpu
from jax.sharding import PartitionSpec as P

SWEEPS = 8
AXES = ("grp", "mem")
PAD = 8
LANES = 128
F32 = jnp.float32
BF16 = jnp.bfloat16
VMEM = pl.BlockSpec(memory_space=pltpu.VMEM)
ANY = pl.BlockSpec(memory_space=pl.ANY)
HBM = pl.BlockSpec(memory_space=pltpu.HBM)


def place():
    members = lax.axis_size("mem")
    return lax.axis_index("grp") * members + lax.axis_index("mem"), lax.axis_size("grp") * members


def in_hbm(array):
    return pltpu.with_memory_space_constraint(array, pltpu.HBM)


def room(mebibytes):
    return pltpu.CompilerParams(vmem_limit_bytes=mebibytes << 20)


def restriction(fine):
    matrix = np.zeros((fine // 2, fine))
    for i in range(fine // 2):
        matrix[i, 2 * i] = 0.5
        matrix[i, 2 * i + 1] = 0.25
        if i > 0:
            matrix[i, 2 * i - 1] = 0.25
    return matrix


def neighbour_sum(n):
    return np.eye(n, k=1) + np.eye(n, k=-1)


def prolongation(coarse):
    matrix = np.zeros((2 * coarse, coarse))
    for i in range(coarse):
        matrix[2 * i, i] = 1.0
        matrix[2 * i + 1, i] += 0.5
        matrix[2 * i + 1, min(i + 1, coarse - 1)] += 0.5
    return matrix


def mode_order(n, devices):
    rows = n // devices
    if rows % 2:
        return np.arange(n)
    half = rows // 2
    low = np.arange(n // 2).reshape(devices, half)
    return np.concatenate([low, n - 1 - low], 1).reshape(-1)


def sine_matrix(n):
    index = np.arange(1, n + 1)
    return np.sqrt(2.0 / (n + 1)) * np.sin(np.pi * np.outer(index, index) / (n + 1))


def split3(x):
    high = x.astype(BF16)
    rest = x - high.astype(F32)
    mid = rest.astype(BF16)
    low = (rest - mid.astype(F32)).astype(BF16)
    return high, mid, low


def split_matrix(matrix, count):
    parts, rest = [], np.asarray(matrix, np.float64)
    for _ in range(count):
        parts.append(rest.astype(jnp.bfloat16))
        rest = rest - parts[-1].astype(np.float64)
    return jnp.asarray(np.stack(parts))


def dot6(matrix_ref, x):
    x = split3(x)
    total = None
    for left, right in ((2, 0), (0, 2), (1, 1), (1, 0), (0, 1), (0, 0)):
        term = jnp.dot(matrix_ref[left], x[right], preferred_element_type=F32)
        total = term if total is None else total + term
    return total


def dot3(parts_ref, first, weights):
    total = None
    for part in (2, 1, 0):
        term = jnp.dot(parts_ref[first + part], weights, preferred_element_type=F32)
        total = term if total is None else total + term
    return total


def restricted_rows(buf, index, start, block):
    def rows(offset):
        return buf[index + (pl.ds(PAD + 2 * start + offset, block, stride=2), slice(None))]

    return rows


def beside(parts, lanes):
    count = len(parts)
    after = [pltpu.roll(part, 1, 1) for part in parts]
    before = [pltpu.roll(part, LANES - 1, 1) for part in parts]
    sums = []
    for c in range(count):
        left = jnp.where(lanes == 0, after[c - 1] if c > 0 else 0.0, after[c])
        right = jnp.where(lanes == LANES - 1, before[c + 1] if c + 1 < count else 0.0, before[c])
        sums.append(left + right)
    return sums


def sent_kernel(
    pot_hbm, src_hbm, rt_hbm,
    near_ref, far_ref, rest_ref, pot, src0,
    src, rt_ref, mid, parts, sem, small_sem,
):
    fine = pot_hbm.shape[1]
    coarse = fine // 2
    blocks = fine // LANES
    cut = fine // 2 + 2 * PAD
    position, _ = place()
    groups = []
    for hbm, plane, buf, index in (
        (pot_hbm, 0, pot, (0,)), (pot_hbm, 1, pot, (1,)), (src_hbm, 1, src, ()), (src_hbm, 0, src0, ()),
    ):
        for first, size in ((0, cut), (cut, fine - cut)):
            group = []
            for c in range(blocks):
                group.append(
                    pltpu.make_async_copy(
                        hbm.at[plane, pl.ds(first, size), pl.ds(c * LANES, LANES)],
                        buf.at[index + (c, pl.ds(PAD + first, size), slice(None))],
                        sem.at[len(groups) * blocks + c],
                    )
                )
            groups.append(group)
    for group in groups[:2]:
        for copy in group:
            copy.start()
    matrix = pltpu.make_async_copy(rt_hbm, rt_ref, small_sem)
    matrix.start()
    for group in groups[2:]:
        for copy in group:
            copy.start()
    edge = jnp.zeros((blocks, PAD, LANES), F32)
    for ref in (pot.at[0], pot.at[1], src, src0):
        ref[:, 0:PAD, :] = edge
        ref[:, PAD + fine : PAD + fine + PAD, :] = edge

    half_not_first = jnp.where(position > 0, 0.5, 0.0).astype(F32)
    block = 32
    lanes = lax.broadcasted_iota(jnp.int32, (block, LANES), 1)
    row_ids = lax.broadcasted_iota(jnp.int32, (block, LANES), 0)

    def chunk(plane, start):
        where = pl.ds(start, block)
        quad, around = [], []
        for c in range(blocks):
            rows = restricted_rows(pot, (plane, c), start, block)
            even = rows(0)
            twice = even + even
            quad.append(twice + (rows(1) + rows(-1)))
            outer = rows(-2) + rows(2)
            if start == 0:
                outer = outer - jnp.where(row_ids == 0, even, 0.0)
            around.append(outer - twice)
        sums = beside(quad, lanes)
        for c in range(blocks):
            columns = pl.ds(c * LANES, LANES)
            whole = (around[c] + sums[c]) - 4.0 * quad[c]
            if plane == 0:
                mid[where, columns] = quad[c]
                rest_ref[where, columns] = whole + half_not_first * quad[c]
                value = quad[c]
            else:
                rows = restricted_rows(src, (c,), start, block)
                even = rows(0)
                source = (even + even) + (rows(1) + rows(-1))
                value = (whole + 0.25 * source) + ((quad[c] + quad[c]) + mid[where, columns])
            for part, piece in enumerate(split3(value)):
                parts[3 * plane + part, where, columns] = piece

    starts = range(0, coarse, block)
    for start in starts:
        if start == 0 or start == coarse // 2:
            for copy in groups[0 if start == 0 else 1]:
                copy.wait()
        chunk(0, start)
    for group in groups[2:6]:
        for copy in group:
            copy.wait()
    matrix.wait()
    down = 0.25 * dot3(parts, 0, rt_ref[...])
    for start in starts:
        chunk(1, start)
    up = 0.25 * dot3(parts, 3, rt_ref[...])
    is_even = lax.rem(position, 2) == 0
    near_ref[...] = jnp.where(is_even, up, down)
    far_ref[...] = jnp.where(is_even, down, up)
    for group in groups[6:]:
        for copy in group:
            copy.wait()


def restriction_matrix(fine):
    return jnp.asarray(restriction(fine).T, BF16)


def sent_stage(potential, source):
    fine = potential.shape[1]
    coarse = fine // 2
    blocks = fine // LANES
    plane = jax.ShapeDtypeStruct((coarse, coarse), F32)
    held = (blocks, fine + 2 * PAD, LANES)
    return pl.pallas_call(
        sent_kernel,
        out_shape=(
            plane,
            plane,
            jax.ShapeDtypeStruct((coarse, fine), F32),
            jax.ShapeDtypeStruct((2,) + held, F32),
            jax.ShapeDtypeStruct(held, F32),
        ),
        in_specs=[HBM] * 3,
        out_specs=(VMEM,) * 5,
        scratch_shapes=[
            pltpu.VMEM(held, F32),
            pltpu.VMEM((fine, coarse), BF16),
            pltpu.VMEM((coarse, fine), F32),
            pltpu.VMEM((6, coarse, fine), BF16),
            pltpu.SemaphoreType.DMA((8 * blocks,)),
            pltpu.SemaphoreType.DMA,
        ],
        compiler_params=room(20),
        name="sent_stage",
    )(in_hbm(potential), in_hbm(source), in_hbm(restriction_matrix(fine)))


def own_kernel(src0, rest_ref, near_ref, far_ref, side_ref, end_hbm, rt_ref, sine_ref, own_ref, sent_ref, end, parts, end_sem):
    coarse, fine = rest_ref.shape
    position, devices = place()
    last = devices - 1
    end_copy = pltpu.make_async_copy(end_hbm.at[jnp.where(position == last, 1, 0)], end, end_sem)
    end_copy.start()
    block = 64
    for c in range(fine // LANES):
        columns = pl.ds(c * LANES, LANES)
        for start in range(0, coarse, block):
            where = pl.ds(start, block)
            rows = restricted_rows(src0, (c,), start, block)
            even = rows(0)
            value = rest_ref[where, columns] + 0.25 * ((even + even) + (rows(1) + rows(-1)))
            for part, piece in enumerate(split3(value)):
                parts[part, where, columns] = piece
    sent_ref[...] = dot6(sine_ref, far_ref[...])
    up = jnp.where(lax.rem(position, 2) == 0, near_ref[...], far_ref[...])
    own_ref[...] = 0.5 * dot3(parts, 0, rt_ref[...]) + up
    side = side_ref[0]
    columns = jnp.transpose(jnp.concatenate([side, side], 0))
    own_ref[0:1, :] += side[0:1]
    own_ref[coarse - 1 : coarse, :] += side[1:2]
    lanes = lax.broadcasted_iota(jnp.int32, (coarse, LANES), 1)
    own_ref[:, 0:LANES] += jnp.where(lanes == 0, columns[:, 2:3], 0.0)
    own_ref[:, coarse - LANES : coarse] += jnp.where(lanes == LANES - 1, columns[:, 3:4], 0.0)
    end_copy.wait()

    @pl.when(jnp.logical_or(position == 0, position == last))
    def _():
        own_ref[...] += end[...]


def own_stage(devices, src0, rest, near, far, side_faces, end_faces):
    coarse, fine = rest.shape
    return pl.pallas_call(
        own_kernel,
        out_shape=(
            jax.ShapeDtypeStruct((coarse, coarse), F32),
            jax.ShapeDtypeStruct((coarse, coarse), F32),
        ),
        in_specs=[VMEM] * 5 + [HBM, VMEM, VMEM],
        out_specs=(VMEM, VMEM),
        scratch_shapes=[
            pltpu.VMEM((coarse, coarse), F32),
            pltpu.VMEM((3, coarse, fine), BF16),
            pltpu.SemaphoreType.DMA,
        ],
        compiler_params=room(12),
        name="own_stage",
    )(src0, rest, near, far, side_faces, in_hbm(end_faces), restriction_matrix(fine), row_transform(coarse, devices))


def rows_kernel(own_ref, near_ref, sine_ref, far_ref, out_ref):
    devices, _, rows, coarse = out_ref.shape
    first = dot6(sine_ref, own_ref[...] + near_ref[...])
    out_ref[:, 0] = first.reshape(devices, rows, coarse)
    out_ref[:, 1] = far_ref[...].reshape(devices, rows, coarse)


def row_transform(coarse, devices):
    return split_matrix(sine_matrix(coarse)[mode_order(coarse, devices)], 3)


def rows_stage(devices, own, near, far):
    coarse = own.shape[0]
    shape = (devices, 2, coarse // devices, coarse)
    return pl.pallas_call(
        rows_kernel,
        out_shape=jax.ShapeDtypeStruct(shape, F32),
        in_specs=[VMEM] * 4,
        out_specs=VMEM,
        compiler_params=room(8),
        name="rows_stage",
    )(own, near, row_transform(coarse, devices), far)


def sweep_kernel(in_ref, alpha_ref, out_ref, values, force):
    planes, _, rows, coarse = in_ref.shape
    paired = rows % 2 == 0
    sixth = 1.0 / 6.0
    shape = (rows, LANES)
    count = coarse // LANES
    lanes = lax.broadcasted_iota(jnp.int32, shape, 1)
    alpha = jnp.broadcast_to(alpha_ref[place()[0]][:, 0:1], shape)
    zero = [jnp.zeros(shape, F32)] * count
    columns = [pl.ds(c * LANES, LANES) for c in range(count)]
    for k in range(planes):
        total = in_ref[k, 0]
        if k % 2 == 0 and k > 0:
            total = total + in_ref[k - 1, 1]
        if k % 2 == 1 and k + 1 < planes:
            total = total + in_ref[k + 1, 1]
        total = total * sixth
        force[k] = total
        values[k] = total

    def held(k):
        return [values[k, :, columns[c]] for c in range(count)]

    def applied(k, under, here, over):
        sums = beside(here, lanes)
        return [
            (force[k, :, columns[c]] + alpha * here[c]) + sixth * ((under[c] + over[c]) + sums[c])
            for c in range(count)
        ]

    def step(counter, carry):
        under, here = zero, held(0)
        for k in range(planes):
            over = held(k + 1) if k + 1 < planes else zero
            for c, value in enumerate(applied(k, under, here, over)):
                values[k, :, columns[c]] = value
            under, here = here, over
        return carry

    lax.fori_loop(0, 2 * SWEEPS - 2, step, 0)

    under, here = zero, held(0)
    for k in range(planes):
        over = held(k + 1) if k + 1 < planes else zero
        black = applied(k, under, here, over)
        for c in range(count):
            mean = 0.5 * (here[c] + black[c])
            swing = 0.5 * (here[c] - black[c])
            swing = jnp.where((lanes + k) % 2 == 0, swing, -swing)
            fields = [mean + pltpu.roll(swing, rows // 2, 0)] if paired else [mean, swing]
            for f, field in enumerate(fields):
                store_solved(out_ref, planes, k, c, f * rows, field)
        under, here = here, over


def packed_sweep_kernel(in_ref, alpha_ref, out_ref, red, black, red_force, black_force):
    planes, _, rows, coarse = in_ref.shape
    slots = planes // 2
    half = rows // 2
    sixth = 1.0 / 6.0
    shape = (rows, LANES)
    count = coarse // LANES
    lanes = lax.broadcasted_iota(jnp.int32, shape, 1)
    first = lax.broadcasted_iota(jnp.int32, shape, 0) < half
    alpha = alpha_ref[place()[0]]
    zero = jnp.zeros(shape, F32)
    columns = [pl.ds(c * LANES, LANES) for c in range(count)]
    signs = [jnp.where((lanes + q) % 2 == 0, 1.0, -1.0) for q in (0, 1)]

    def forcing(k, c):
        total = in_ref[k, 0, :, columns[c]]
        if k % 2 == 0 and k > 0:
            total = total + in_ref[k - 1, 1, :, columns[c]]
        if k % 2 == 1 and k + 1 < planes:
            total = total + in_ref[k + 1, 1, :, columns[c]]
        return total

    def swapped(x):
        return pltpu.roll(x, half, 0)

    for q in range(slots):
        for c in range(count):
            one, two = forcing(q, c), forcing(q + slots, c)
            low = jnp.where(first, one, swapped(two)) * (0.5 * sixth)
            high = jnp.where(first, swapped(one), two) * (0.5 * sixth * signs[q % 2])
            red_force[q, :, columns[c]] = low + high
            black_force[q, :, columns[c]] = low - high
            red[q, :, columns[c]] = low + high

    def update(target, force, other):
        def held(q):
            return [other[q, :, columns[c]] for c in range(count)]

        here, end = held(0), held(slots - 1)
        under = [jnp.where(first, zero, swapped(x)) for x in end]
        beyond = [jnp.where(first, swapped(x), zero) for x in here]
        for q in range(slots):
            over = held(q + 1) if q + 1 < slots else beyond
            sums = beside(here, lanes)
            for c in range(count):
                target[q, :, columns[c]] = (force[q, :, columns[c]] + alpha * here[c]) + sixth * (
                    (under[c] + over[c]) + sums[c]
                )
            under, here = here, over

    update(black, black_force, red)

    def sweep(counter, carry):
        update(red, red_force, black)
        update(black, black_force, red)
        return carry

    lax.fori_loop(0, SWEEPS - 1, sweep, 0)

    for q in range(slots):
        for c in range(count):
            on_red, on_black = red[q, :, columns[c]], black[q, :, columns[c]]
            low = on_red + on_black
            high = signs[q % 2] * (on_red - on_black)
            store_solved(out_ref, planes, q, c, 0, jnp.where(first, low, swapped(high)))
            store_solved(out_ref, planes, q + slots, c, 0, jnp.where(first, swapped(low), high))


def store_solved(out_ref, planes, k, c, first_row, field):
    rows = field.shape[0]
    coarse = out_ref.shape[2] // 3 * 2
    where = pl.ds(first_row, rows)
    out_ref[k, where, pl.ds(c * LANES, LANES)] = field
    if k >= 2 and k % 2 == 0 or k == planes - 1:
        half = coarse // 2
        before = k - 2 if k < planes - 1 else k - 1
        side = c * LANES // half
        out_ref[before + side, where, pl.ds(coarse + c * LANES - side * half, LANES)] = field


def sweep_stage(received):
    devices, _, rows, coarse = received.shape
    packed = rows == 8 and devices % 4 == 0
    fields = 1 if rows % 2 == 0 else 2
    modes = (mode_order(coarse, devices) + 1).reshape(devices, rows)
    if packed:
        modes = np.concatenate([modes[:, : rows // 2]] * 2, 1)
    alpha = np.cos(np.pi * modes / (coarse + 1)) / 3.0
    table = jnp.asarray(np.tile(alpha[:, :, None], (1, 1, LANES)), F32)
    shape = (devices // 2 if packed else devices, rows, coarse)
    return pl.pallas_call(
        packed_sweep_kernel if packed else sweep_kernel,
        out_shape=jax.ShapeDtypeStruct((devices, fields * rows, coarse + coarse // 2), F32),
        in_specs=[VMEM, VMEM],
        out_specs=VMEM,
        scratch_shapes=[pltpu.VMEM(shape, F32)] * (4 if packed else 2),
        compiler_params=room(8 if rows % 8 == 0 else 24),
        name="sweep_stage",
    )(received, table)


def back_kernel(in_ref, back_ref, corr_ref, swap_ref, extra_ref):
    devices, held, width = in_ref.shape
    coarse = corr_ref.shape[0]
    rows = coarse // devices
    fields = held // rows
    position, _ = place()

    def product(first, size):
        total = None
        for f in range(fields):
            part = in_ref[:, f * rows : (f + 1) * rows, first : first + size].reshape(coarse, size)
            high = part.astype(BF16)
            low = (part - high.astype(F32)).astype(BF16)
            for left, right in ((1, high), (0, low), (0, high)):
                term = jnp.dot(back_ref[2 * f + left], right, preferred_element_type=F32)
                total = term if total is None else total + term
        return total

    both = product(0, width)
    own, extra = both[:, 0:coarse], both[:, coarse:]
    corr_ref[...] = own
    extra_ref[...] = extra
    is_even = lax.rem(position, 2) == 0

    @pl.when(is_even)
    def _():
        swap_ref[:, 0 : width - coarse] = extra
        swap_ref[:, width - coarse :] = extra

    @pl.when(jnp.logical_not(is_even))
    def _():
        swap_ref[...] = own


def back_stage(coarse, received):
    devices, held, width = received.shape
    rows = coarse // devices
    order = mode_order(coarse, devices)
    sine = sine_matrix(coarse)
    back = [sine[order].T]
    if held > rows:
        back.append(sine[coarse - 1 - order].T)
    return pl.pallas_call(
        back_kernel,
        out_shape=(
            jax.ShapeDtypeStruct((coarse, coarse), F32),
            jax.ShapeDtypeStruct((coarse, coarse), F32),
            jax.ShapeDtypeStruct((coarse, width - coarse), F32),
        ),
        in_specs=[VMEM, VMEM],
        out_specs=(VMEM,) * 3,
        compiler_params=room(8),
        name="back_stage",
    )(received, jnp.concatenate([split_matrix(matrix, 2) for matrix in back]))


def add_prolonged(value, pt_ref, pot, plane, out_hbm, out, parts, wide, sem):
    coarse = value.shape[0]
    fine = 2 * coarse
    block = 64
    for part, piece in enumerate(split3(value)):
        parts[part] = piece
    stores = []
    for n in range(0, fine, coarse):
        wide[0:coarse, :] = dot3(parts, 0, pt_ref[:, n : n + coarse])
        wide[coarse : coarse + 1, :] = wide[coarse - 1 : coarse, :]
        for c in range(n // LANES, (n + coarse) // LANES):
            lanes = pl.ds(c * LANES - n, LANES)
            for start in range(0, coarse, block):
                here = wide[pl.ds(start, block), lanes]
                after = wide[pl.ds(start + 1, block), lanes]
                for odd, value in ((0, here), (1, 0.5 * (here + after))):
                    old = pot[plane, c, pl.ds(PAD + 2 * start + odd, block, stride=2), :]
                    out[c, pl.ds(2 * start + odd, block, stride=2), :] = old + value
            stores.append(
                pltpu.make_async_copy(out.at[c], out_hbm.at[plane, :, pl.ds(c * LANES, LANES)], sem.at[c])
            )
            stores[-1].start()
    for store in stores:
        store.wait()


def even_kernel(own_ref, pt_ref, pot, out_hbm, corr_hbm, out, parts, wide, sem, corr_sem):
    copy = pltpu.make_async_copy(own_ref, corr_hbm.at[0], corr_sem)
    copy.start()
    add_prolonged(own_ref[...], pt_ref, pot, 0, out_hbm, out, parts, wide, sem)
    copy.wait()


def odd_kernel(own_ref, swapped_ref, extra_ref, pt_ref, pot, held_hbm, out_hbm, out, parts, wide, sem):
    position, devices = place()
    own = own_ref[...]
    swapped = swapped_ref[...]
    half = extra_ref.shape[1]
    is_even = lax.rem(position, 2) == 0
    right = jnp.where(is_even, swapped[:, half:], extra_ref[...])
    above = jnp.concatenate([swapped[:, :half], right], 1)
    above = jnp.where(position == devices - 1, own, above)
    add_prolonged(0.5 * (own + above), pt_ref, pot, 1, out_hbm, out, parts, wide, sem)


def plane_stage(name, kernel, operands, pot, held):
    coarse = operands[0].shape[0]
    fine = 2 * coarse
    pt = jnp.asarray(prolongation(coarse).T, BF16)
    arguments = list(operands) + [pt, pot]
    specs = [VMEM] * len(arguments)
    scratch = [
        pltpu.VMEM((fine // LANES, fine, LANES), F32),
        pltpu.VMEM((3, coarse, coarse), BF16),
        pltpu.VMEM((coarse + PAD, coarse), F32),
        pltpu.SemaphoreType.DMA((fine // LANES,)),
    ]
    outs = [jax.ShapeDtypeStruct((2, fine, fine), F32)]
    if held is None:
        outs.append(jax.ShapeDtypeStruct((1, coarse, coarse), F32))
        scratch.append(pltpu.SemaphoreType.DMA)
    else:
        arguments.append(held)
        specs.append(ANY)
    return pl.pallas_call(
        kernel,
        out_shape=outs,
        in_specs=specs,
        out_specs=[HBM] * len(outs),
        scratch_shapes=scratch,
        input_output_aliases={} if held is None else {len(arguments) - 1: 0},
        compiler_params=room(8),
        name=name,
    )(*arguments)


def per_device(potential, source, side_faces, end_faces):
    devices = lax.axis_size("grp") * lax.axis_size("mem")
    coarse = side_faces.shape[2]
    in_chip = [(i, i ^ 1) for i in range(devices)]
    near, far, rest, pot, src0 = sent_stage(potential, source)
    arrived = lax.ppermute(near, AXES, in_chip)
    own, far = own_stage(devices, src0, rest, near, far, side_faces, end_faces)
    sent = rows_stage(devices, own, arrived, far)
    received = lax.all_to_all(sent, AXES, 0, 0, tiled=True)
    solved = sweep_stage(received)
    returned = lax.all_to_all(solved, AXES, 0, 0, tiled=True)
    own, swapped, extra = back_stage(coarse, returned)
    swapped = lax.ppermute(swapped, AXES, in_chip)
    corrected, correction = plane_stage("even_stage", even_kernel, (own,), pot, None)
    (corrected,) = plane_stage("odd_stage", odd_kernel, (own, swapped, extra), pot, corrected)
    return corrected, correction


def solution(mesh):
    split = P(AXES, None, None)
    return jax.shard_map(
        per_device,
        mesh=mesh,
        in_specs=(split, split, split, P()),
        out_specs=(split, split),
        check_vma=False,
    )
```

```python
import jax
import jax.numpy as jnp
import numpy as np
from jax import lax
from jax.experimental import pallas as pl
from jax.experimental.pallas import tpu as pltpu
from jax.sharding import PartitionSpec as P

SWEEPS = 8
AXES = ("grp", "mem")
PAD = 8
LANES = 128
F32 = jnp.float32
BF16 = jnp.bfloat16
VMEM = pl.BlockSpec(memory_space=pltpu.VMEM)
ANY = pl.BlockSpec(memory_space=pl.ANY)
HBM = pl.BlockSpec(memory_space=pltpu.HBM)


def place():
    members = lax.axis_size("mem")
    return lax.axis_index("grp") * members + lax.axis_index("mem"), lax.axis_size("grp") * members


def in_hbm(array):
    return pltpu.with_memory_space_constraint(array, pltpu.HBM)


def room(mebibytes):
    return pltpu.CompilerParams(vmem_limit_bytes=mebibytes << 20)


def restriction(fine):
    matrix = np.zeros((fine // 2, fine))
    for i in range(fine // 2):
        matrix[i, 2 * i] = 0.5
        matrix[i, 2 * i + 1] = 0.25
        if i > 0:
            matrix[i, 2 * i - 1] = 0.25
    return matrix


def neighbour_sum(n):
    return np.eye(n, k=1) + np.eye(n, k=-1)


def prolongation(coarse):
    matrix = np.zeros((2 * coarse, coarse))
    for i in range(coarse):
        matrix[2 * i, i] = 1.0
        matrix[2 * i + 1, i] += 0.5
        matrix[2 * i + 1, min(i + 1, coarse - 1)] += 0.5
    return matrix


def mode_order(n, devices):
    rows = n // devices
    if rows % 2:
        return np.arange(n)
    half = rows // 2
    low = np.arange(n // 2).reshape(devices, half)
    return np.concatenate([low, n - 1 - low], 1).reshape(-1)


def sine_matrix(n):
    index = np.arange(1, n + 1)
    return np.sqrt(2.0 / (n + 1)) * np.sin(np.pi * np.outer(index, index) / (n + 1))


def split3(x):
    high = x.astype(BF16)
    rest = x - high.astype(F32)
    mid = rest.astype(BF16)
    low = (rest - mid.astype(F32)).astype(BF16)
    return high, mid, low


def split_matrix(matrix, count):
    parts, rest = [], np.asarray(matrix, np.float64)
    for _ in range(count):
        parts.append(rest.astype(jnp.bfloat16))
        rest = rest - parts[-1].astype(np.float64)
    return jnp.asarray(np.stack(parts))


def dot6(matrix_ref, x):
    x = split3(x)
    total = None
    for left, right in ((2, 0), (0, 2), (1, 1), (1, 0), (0, 1), (0, 0)):
        term = jnp.dot(matrix_ref[left], x[right], preferred_element_type=F32)
        total = term if total is None else total + term
    return total


def dot3(parts_ref, first, weights):
    total = None
    for part in (2, 1, 0):
        term = jnp.dot(parts_ref[first + part], weights, preferred_element_type=F32)
        total = term if total is None else total + term
    return total


def restricted_rows(buf, index, start, block):
    def rows(offset):
        return buf[index + (pl.ds(PAD + 2 * start + offset, block, stride=2), slice(None))]

    return rows


def beside(parts, lanes):
    count = len(parts)
    after = [pltpu.roll(part, 1, 1) for part in parts]
    before = [pltpu.roll(part, LANES - 1, 1) for part in parts]
    sums = []
    for c in range(count):
        left = jnp.where(lanes == 0, after[c - 1] if c > 0 else 0.0, after[c])
        right = jnp.where(lanes == LANES - 1, before[c + 1] if c + 1 < count else 0.0, before[c])
        sums.append(left + right)
    return sums


def around(rows, even, row_ids, start):
    outer = rows(-2) + rows(2)
    if start == 0:
        outer = outer - jnp.where(row_ids == 0, even, 0.0)
    return outer - (even + even)


def in_plane(quad, outer, lanes):
    sums = beside(quad, lanes)
    return [(outer[c] + sums[c]) - 4.0 * quad[c] for c in range(len(quad))]


def sent_kernel(
    pot_hbm, src_hbm, end_hbm, rt_hbm, sine_hbm,
    near_ref, far_ref, pot, src0, end, rt_ref, sine_ref,
    src, mid, parts, sem, small_sem,
):
    fine = pot_hbm.shape[1]
    coarse = fine // 2
    blocks = fine // LANES
    cut = fine // 2 + 2 * PAD
    position, devices = place()
    groups = []
    for hbm, plane, buf, index in (
        (pot_hbm, 0, pot, (0,)), (pot_hbm, 1, pot, (1,)), (src_hbm, 1, src, ()), (src_hbm, 0, src0, ()),
    ):
        for first, size in ((0, fine),):
            group = []
            for c in range(blocks):
                group.append(
                    pltpu.make_async_copy(
                        hbm.at[plane, pl.ds(first, size), pl.ds(c * LANES, LANES)],
                        buf.at[index + (c, pl.ds(PAD + first, size), slice(None))],
                        sem.at[len(groups) * blocks + c],
                    )
                )
            groups.append(group)
    for group in groups[:1]:
        for copy in group:
            copy.start()
    matrix = pltpu.make_async_copy(rt_hbm, rt_ref, small_sem.at[0])
    matrix.start()
    for group in groups[1:3]:
        for copy in group:
            copy.start()
    for copy in groups[3]:
        copy.start(priority=1)
    sine = pltpu.make_async_copy(sine_hbm, sine_ref, small_sem.at[1])
    sine.start()
    last = devices - 1
    at_end = jnp.logical_or(position == 0, position == last)
    end_copy = pltpu.make_async_copy(end_hbm.at[jnp.where(position == last, 1, 0)], end, small_sem.at[2])

    @pl.when(at_end)
    def _():
        end_copy.start()

    edge = jnp.zeros((blocks, PAD, LANES), F32)
    for ref in (pot.at[0], pot.at[1], src, src0):
        ref[:, 0:PAD, :] = edge
        ref[:, PAD + fine : PAD + fine + PAD, :] = edge

    block = 32
    lanes = lax.broadcasted_iota(jnp.int32, (block, LANES), 1)
    row_ids = lax.broadcasted_iota(jnp.int32, (block, LANES), 0)

    def chunk(plane, start):
        where = pl.ds(start, block)
        quad, whole = [], []
        for c in range(blocks):
            rows = restricted_rows(pot, (plane, c), start, block)
            even = rows(0)
            quad.append((even + even) + (rows(1) + rows(-1)))
            if plane == 1:
                whole.append(around(rows, even, row_ids, start))
        if plane == 1:
            whole = in_plane(quad, whole, lanes)
        for c in range(blocks):
            columns = pl.ds(c * LANES, LANES)
            if plane == 0:
                mid[where, columns] = quad[c]
                pieces(0, where, columns, quad[c])
            else:
                rows = restricted_rows(src, (c,), start, block)
                even = rows(0)
                source = (even + even) + (rows(1) + rows(-1))
                value = (whole[c] + 0.25 * source) + ((quad[c] + quad[c]) + mid[where, columns])
                pieces(3, where, columns, value)

    def pieces(first, where, columns, value):
        for part, piece in enumerate(split3(value)):
            parts[first + part, where, columns] = piece

    starts = range(0, coarse, block)
    for copy in groups[0]:
        copy.wait()
    for start in starts:
        chunk(0, start)
    for group in groups[1:3]:
        for copy in group:
            copy.wait()
    matrix.wait()
    for start in starts:
        chunk(1, start)
    down = 0.25 * dot3(parts, 0, rt_ref[...])
    up = 0.25 * dot3(parts, 3, rt_ref[...])
    is_even = lax.rem(position, 2) == 0
    near_ref[...] = jnp.where(is_even, up, down)
    far_ref[...] = jnp.where(is_even, down, up)
    for group in groups[3:]:
        for copy in group:
            copy.wait()
    sine.wait()

    @pl.when(at_end)
    def _():
        end_copy.wait()


def restriction_matrix(fine):
    return jnp.asarray(restriction(fine).T, BF16)


def sent_stage(devices, potential, source, end_faces):
    fine = potential.shape[1]
    coarse = fine // 2
    blocks = fine // LANES
    plane = jax.ShapeDtypeStruct((coarse, coarse), F32)
    held = (blocks, fine + 2 * PAD, LANES)
    return pl.pallas_call(
        sent_kernel,
        out_shape=(
            plane,
            plane,
            jax.ShapeDtypeStruct((2,) + held, F32),
            jax.ShapeDtypeStruct(held, F32),
            plane,
            jax.ShapeDtypeStruct((fine, coarse), BF16),
            jax.ShapeDtypeStruct((3, coarse, coarse), BF16),
        ),
        in_specs=[HBM] * 5,
        out_specs=(VMEM,) * 7,
        scratch_shapes=[
            pltpu.VMEM(held, F32),
            pltpu.VMEM((coarse, fine), F32),
            pltpu.VMEM((6, coarse, fine), BF16),
            pltpu.SemaphoreType.DMA((8 * blocks,)),
            pltpu.SemaphoreType.DMA((3,)),
        ],
        compiler_params=room(20),
        name="sent_stage",
    )(
        in_hbm(potential), in_hbm(source), in_hbm(end_faces),
        in_hbm(restriction_matrix(fine)), in_hbm(row_transform(coarse, devices)),
    )


def own_kernel(src0, pot, near_ref, far_ref, side_ref, end, rt_ref, sine_ref, own_ref, sent_ref, parts):
    fine, coarse = rt_ref.shape
    position, devices = place()
    last = devices - 1
    half_not_first = jnp.where(position > 0, 0.5, 0.0).astype(F32)
    block = 32
    shape = (block, LANES)
    lanes = lax.broadcasted_iota(jnp.int32, shape, 1)
    row_ids = lax.broadcasted_iota(jnp.int32, shape, 0)
    for start in range(0, coarse, block):
        where = pl.ds(start, block)
        quad, outer = [], []
        for c in range(fine // LANES):
            rows = restricted_rows(pot, (0, c), start, block)
            even = rows(0)
            quad.append((even + even) + (rows(1) + rows(-1)))
            outer.append(around(rows, even, row_ids, start))
        whole = in_plane(quad, outer, lanes)
        for c in range(fine // LANES):
            rows = restricted_rows(src0, (c,), start, block)
            even = rows(0)
            source = (even + even) + (rows(1) + rows(-1))
            value = (whole[c] + half_not_first * quad[c]) + 0.25 * source
            for part, piece in enumerate(split3(value)):
                parts[part, where, pl.ds(c * LANES, LANES)] = piece
    sent_ref[...] = dot6(sine_ref, far_ref[...])
    up = jnp.where(lax.rem(position, 2) == 0, near_ref[...], far_ref[...])
    own_ref[...] = 0.5 * dot3(parts, 0, rt_ref[...]) + up
    side = side_ref[0]
    columns = jnp.transpose(jnp.concatenate([side, side], 0))
    own_ref[0:1, :] += side[0:1]
    own_ref[coarse - 1 : coarse, :] += side[1:2]
    lanes = lax.broadcasted_iota(jnp.int32, (coarse, LANES), 1)
    own_ref[:, 0:LANES] += jnp.where(lanes == 0, columns[:, 2:3], 0.0)
    own_ref[:, coarse - LANES : coarse] += jnp.where(lanes == LANES - 1, columns[:, 3:4], 0.0)

    @pl.when(jnp.logical_or(position == 0, position == last))
    def _():
        own_ref[...] += end[...]


def own_stage(src0, pot, near, far, side_faces, end, rt, sine):
    fine, coarse = rt.shape
    return pl.pallas_call(
        own_kernel,
        out_shape=(
            jax.ShapeDtypeStruct((coarse, coarse), F32),
            jax.ShapeDtypeStruct((coarse, coarse), F32),
        ),
        in_specs=[VMEM] * 8,
        out_specs=(VMEM, VMEM),
        scratch_shapes=[pltpu.VMEM((3, coarse, fine), BF16)],
        compiler_params=room(12),
        name="own_stage",
    )(src0, pot, near, far, side_faces, end, rt, sine)


def rows_kernel(own_ref, near_ref, sine_ref, far_ref, out_ref):
    devices, _, rows, coarse = out_ref.shape
    first = dot6(sine_ref, own_ref[...] + near_ref[...])
    out_ref[:, 0] = first.reshape(devices, rows, coarse)
    out_ref[:, 1] = far_ref[...].reshape(devices, rows, coarse)


def row_transform(coarse, devices):
    return split_matrix(sine_matrix(coarse)[mode_order(coarse, devices)], 3)


def rows_stage(devices, own, near, far, sine):
    coarse = own.shape[0]
    shape = (devices, 2, coarse // devices, coarse)
    return pl.pallas_call(
        rows_kernel,
        out_shape=jax.ShapeDtypeStruct(shape, F32),
        in_specs=[VMEM] * 4,
        out_specs=VMEM,
        compiler_params=room(8),
        name="rows_stage",
    )(own, near, sine, far)


def sweep_kernel(in_ref, alpha_ref, out_ref, values, force):
    planes, _, rows, coarse = in_ref.shape
    paired = rows % 2 == 0
    sixth = 1.0 / 6.0
    shape = (rows, LANES)
    count = coarse // LANES
    lanes = lax.broadcasted_iota(jnp.int32, shape, 1)
    alpha = jnp.broadcast_to(alpha_ref[place()[0]][:, 0:1], shape)
    zero = [jnp.zeros(shape, F32)] * count
    columns = [pl.ds(c * LANES, LANES) for c in range(count)]
    for k in range(planes):
        total = in_ref[k, 0]
        if k % 2 == 0 and k > 0:
            total = total + in_ref[k - 1, 1]
        if k % 2 == 1 and k + 1 < planes:
            total = total + in_ref[k + 1, 1]
        total = total * sixth
        force[k] = total
        values[k] = total

    def held(k):
        return [values[k, :, columns[c]] for c in range(count)]

    def applied(k, under, here, over):
        sums = beside(here, lanes)
        return [
            (force[k, :, columns[c]] + alpha * here[c]) + sixth * ((under[c] + over[c]) + sums[c])
            for c in range(count)
        ]

    def step(counter, carry):
        under, here = zero, held(0)
        for k in range(planes):
            over = held(k + 1) if k + 1 < planes else zero
            for c, value in enumerate(applied(k, under, here, over)):
                values[k, :, columns[c]] = value
            under, here = here, over
        return carry

    lax.fori_loop(0, 2 * SWEEPS - 2, step, 0)

    under, here = zero, held(0)
    for k in range(planes):
        over = held(k + 1) if k + 1 < planes else zero
        black = applied(k, under, here, over)
        for c in range(count):
            mean = 0.5 * (here[c] + black[c])
            swing = 0.5 * (here[c] - black[c])
            swing = jnp.where((lanes + k) % 2 == 0, swing, -swing)
            fields = [mean + pltpu.roll(swing, rows // 2, 0)] if paired else [mean, swing]
            for f, field in enumerate(fields):
                store_solved(out_ref, planes, k, c, f * rows, field)
        under, here = here, over


def packed_sweep_kernel(in_ref, alpha_ref, out_ref, red, black, red_force, black_force):
    planes, _, rows, coarse = in_ref.shape
    slots = planes // 2
    half = rows // 2
    sixth = 1.0 / 6.0
    shape = (rows, LANES)
    count = coarse // LANES
    lanes = lax.broadcasted_iota(jnp.int32, shape, 1)
    first = lax.broadcasted_iota(jnp.int32, shape, 0) < half
    alpha = alpha_ref[place()[0]]
    zero = jnp.zeros(shape, F32)
    columns = [pl.ds(c * LANES, LANES) for c in range(count)]
    signs = [jnp.where((lanes + q) % 2 == 0, 1.0, -1.0) for q in (0, 1)]

    def forcing(k, c):
        total = in_ref[k, 0, :, columns[c]]
        if k % 2 == 0 and k > 0:
            total = total + in_ref[k - 1, 1, :, columns[c]]
        if k % 2 == 1 and k + 1 < planes:
            total = total + in_ref[k + 1, 1, :, columns[c]]
        return total

    def swapped(x):
        return pltpu.roll(x, half, 0)

    for q in range(slots):
        for c in range(count):
            one, two = forcing(q, c), forcing(q + slots, c)
            low = jnp.where(first, one, swapped(two)) * (0.5 * sixth)
            high = jnp.where(first, swapped(one), two) * (0.5 * sixth * signs[q % 2])
            red_force[q, :, columns[c]] = low + high
            black_force[q, :, columns[c]] = low - high
            red[q, :, columns[c]] = low + high

    def update(target, force, other):
        def held(q):
            return [other[q, :, columns[c]] for c in range(count)]

        here, end = held(0), held(slots - 1)
        under = [jnp.where(first, zero, swapped(x)) for x in end]
        beyond = [jnp.where(first, swapped(x), zero) for x in here]
        for q in range(slots):
            over = held(q + 1) if q + 1 < slots else beyond
            sums = beside(here, lanes)
            for c in range(count):
                target[q, :, columns[c]] = (force[q, :, columns[c]] + alpha * here[c]) + sixth * (
                    (under[c] + over[c]) + sums[c]
                )
            under, here = here, over

    update(black, black_force, red)

    def sweep(counter, carry):
        update(red, red_force, black)
        update(black, black_force, red)
        return carry

    lax.fori_loop(0, SWEEPS - 1, sweep, 0)

    for q in range(slots):
        for c in range(count):
            on_red, on_black = red[q, :, columns[c]], black[q, :, columns[c]]
            low = on_red + on_black
            high = signs[q % 2] * (on_red - on_black)
            store_solved(out_ref, planes, q, c, 0, jnp.where(first, low, swapped(high)))
            store_solved(out_ref, planes, q + slots, c, 0, jnp.where(first, swapped(low), high))


def store_solved(out_ref, planes, k, c, first_row, field):
    rows = field.shape[0]
    coarse = out_ref.shape[2] // 3 * 2
    where = pl.ds(first_row, rows)
    out_ref[k, where, pl.ds(c * LANES, LANES)] = field
    if k >= 2 and k % 2 == 0 or k == planes - 1:
        half = coarse // 2
        before = k - 2 if k < planes - 1 else k - 1
        side = c * LANES // half
        out_ref[before + side, where, pl.ds(coarse + c * LANES - side * half, LANES)] = field


def sweep_stage(received):
    devices, _, rows, coarse = received.shape
    packed = rows == 8 and devices % 4 == 0
    fields = 1 if rows % 2 == 0 else 2
    modes = (mode_order(coarse, devices) + 1).reshape(devices, rows)
    if packed:
        modes = np.concatenate([modes[:, : rows // 2]] * 2, 1)
    alpha = np.cos(np.pi * modes / (coarse + 1)) / 3.0
    table = jnp.asarray(np.tile(alpha[:, :, None], (1, 1, LANES)), F32)
    shape = (devices // 2 if packed else devices, rows, coarse)
    return pl.pallas_call(
        packed_sweep_kernel if packed else sweep_kernel,
        out_shape=jax.ShapeDtypeStruct((devices, fields * rows, coarse + coarse // 2), F32),
        in_specs=[VMEM, VMEM],
        out_specs=VMEM,
        scratch_shapes=[pltpu.VMEM(shape, F32)] * (4 if packed else 2),
        compiler_params=room(8 if rows % 8 == 0 else 24),
        name="sweep_stage",
    )(received, table)


def back_kernel(in_ref, back_ref, corr_ref, swap_ref, extra_ref):
    devices, held, width = in_ref.shape
    coarse = corr_ref.shape[0]
    rows = coarse // devices
    fields = held // rows
    position, _ = place()

    def product(first, size):
        total = None
        for f in range(fields):
            part = in_ref[:, f * rows : (f + 1) * rows, first : first + size].reshape(coarse, size)
            high = part.astype(BF16)
            low = (part - high.astype(F32)).astype(BF16)
            for left, right in ((1, high), (0, low), (0, high)):
                term = jnp.dot(back_ref[2 * f + left], right, preferred_element_type=F32)
                total = term if total is None else total + term
        return total

    both = product(0, width)
    own, extra = both[:, 0:coarse], both[:, coarse:]
    corr_ref[...] = own
    extra_ref[...] = extra
    is_even = lax.rem(position, 2) == 0

    @pl.when(is_even)
    def _():
        swap_ref[:, 0 : width - coarse] = extra
        swap_ref[:, width - coarse :] = extra

    @pl.when(jnp.logical_not(is_even))
    def _():
        swap_ref[...] = own


def back_stage(coarse, received):
    devices, held, width = received.shape
    rows = coarse // devices
    order = mode_order(coarse, devices)
    sine = sine_matrix(coarse)
    back = [sine[order].T]
    if held > rows:
        back.append(sine[coarse - 1 - order].T)
    return pl.pallas_call(
        back_kernel,
        out_shape=(
            jax.ShapeDtypeStruct((coarse, coarse), F32),
            jax.ShapeDtypeStruct((coarse, coarse), F32),
            jax.ShapeDtypeStruct((coarse, width - coarse), F32),
        ),
        in_specs=[VMEM, VMEM],
        out_specs=(VMEM,) * 3,
        compiler_params=room(8),
        name="back_stage",
    )(received, jnp.concatenate([split_matrix(matrix, 2) for matrix in back]))


def add_prolonged(value, pt_ref, pot, plane, out_hbm, out, parts, wide, sem):
    coarse = value.shape[0]
    fine = 2 * coarse
    block = 64
    for part, piece in enumerate(split3(value)):
        parts[part] = piece
    stores = []
    for n in range(0, fine, coarse):
        wide[0:coarse, :] = dot3(parts, 0, pt_ref[:, n : n + coarse])
        wide[coarse : coarse + 1, :] = wide[coarse - 1 : coarse, :]
        for c in range(n // LANES, (n + coarse) // LANES):
            lanes = pl.ds(c * LANES - n, LANES)
            for start in range(0, coarse, block):
                here = wide[pl.ds(start, block), lanes]
                after = wide[pl.ds(start + 1, block), lanes]
                for odd, value in ((0, here), (1, 0.5 * (here + after))):
                    old = pot[plane, c, pl.ds(PAD + 2 * start + odd, block, stride=2), :]
                    out[c, pl.ds(2 * start + odd, block, stride=2), :] = old + value
            stores.append(
                pltpu.make_async_copy(out.at[c], out_hbm.at[plane, :, pl.ds(c * LANES, LANES)], sem.at[c])
            )
            stores[-1].start()
    for store in stores:
        store.wait()


def even_kernel(own_ref, pt_ref, pot, out_hbm, corr_hbm, out, parts, wide, sem, corr_sem):
    copy = pltpu.make_async_copy(own_ref, corr_hbm.at[0], corr_sem)
    copy.start()
    add_prolonged(own_ref[...], pt_ref, pot, 0, out_hbm, out, parts, wide, sem)
    copy.wait()


def odd_kernel(own_ref, swapped_ref, extra_ref, pt_ref, pot, held_hbm, out_hbm, out, parts, wide, sem):
    position, devices = place()
    own = own_ref[...]
    swapped = swapped_ref[...]
    half = extra_ref.shape[1]
    is_even = lax.rem(position, 2) == 0
    right = jnp.where(is_even, swapped[:, half:], extra_ref[...])
    above = jnp.concatenate([swapped[:, :half], right], 1)
    above = jnp.where(position == devices - 1, own, above)
    add_prolonged(0.5 * (own + above), pt_ref, pot, 1, out_hbm, out, parts, wide, sem)


def plane_stage(name, kernel, operands, pot, held):
    coarse = operands[0].shape[0]
    fine = 2 * coarse
    pt = jnp.asarray(prolongation(coarse).T, BF16)
    arguments = list(operands) + [pt, pot]
    specs = [VMEM] * len(arguments)
    scratch = [
        pltpu.VMEM((fine // LANES, fine, LANES), F32),
        pltpu.VMEM((3, coarse, coarse), BF16),
        pltpu.VMEM((coarse + PAD, coarse), F32),
        pltpu.SemaphoreType.DMA((fine // LANES,)),
    ]
    outs = [jax.ShapeDtypeStruct((2, fine, fine), F32)]
    if held is None:
        outs.append(jax.ShapeDtypeStruct((1, coarse, coarse), F32))
        scratch.append(pltpu.SemaphoreType.DMA)
    else:
        arguments.append(held)
        specs.append(ANY)
    return pl.pallas_call(
        kernel,
        out_shape=outs,
        in_specs=specs,
        out_specs=[HBM] * len(outs),
        scratch_shapes=scratch,
        input_output_aliases={} if held is None else {len(arguments) - 1: 0},
        compiler_params=room(8),
        name=name,
    )(*arguments)


def per_device(potential, source, side_faces, end_faces):
    devices = lax.axis_size("grp") * lax.axis_size("mem")
    coarse = side_faces.shape[2]
    in_chip = [(i, i ^ 1) for i in range(devices)]
    near, far, pot, src0, end, rt, sine = sent_stage(devices, potential, source, end_faces)
    arrived = lax.ppermute(near, AXES, in_chip)
    own, far = own_stage(src0, pot, near, far, side_faces, end, rt, sine)
    sent = rows_stage(devices, own, arrived, far, sine)
    received = lax.all_to_all(sent, AXES, 0, 0, tiled=True)
    solved = sweep_stage(received)
    returned = lax.all_to_all(solved, AXES, 0, 0, tiled=True)
    own, swapped, extra = back_stage(coarse, returned)
    swapped = lax.ppermute(swapped, AXES, in_chip)
    corrected, correction = plane_stage("even_stage", even_kernel, (own,), pot, None)
    (corrected,) = plane_stage("odd_stage", odd_kernel, (own, swapped, extra), pot, corrected)
    return corrected, correction


def solution(mesh):
    split = P(AXES, None, None)
    return jax.shard_map(
        per_device,
        mesh=mesh,
        in_specs=(split, split, split, P()),
        out_specs=(split, split),
        check_vma=False,
    )
```

```python
import jax
import jax.numpy as jnp
import numpy as np
from jax import lax
from jax.experimental import pallas as pl
from jax.experimental.pallas import tpu as pltpu
from jax.sharding import PartitionSpec as P

SWEEPS = 8
AXES = ("grp", "mem")
PAD = 8
LANES = 128
F32 = jnp.float32
BF16 = jnp.bfloat16
VMEM = pl.BlockSpec(memory_space=pltpu.VMEM)
ANY = pl.BlockSpec(memory_space=pl.ANY)
HBM = pl.BlockSpec(memory_space=pltpu.HBM)


def place():
    members = lax.axis_size("mem")
    return lax.axis_index("grp") * members + lax.axis_index("mem"), lax.axis_size("grp") * members


def in_hbm(array):
    return pltpu.with_memory_space_constraint(array, pltpu.HBM)


def room(mebibytes):
    return pltpu.CompilerParams(vmem_limit_bytes=mebibytes << 20)


def restriction(fine):
    matrix = np.zeros((fine // 2, fine))
    for i in range(fine // 2):
        matrix[i, 2 * i] = 0.5
        matrix[i, 2 * i + 1] = 0.25
        if i > 0:
            matrix[i, 2 * i - 1] = 0.25
    return matrix


def neighbour_sum(n):
    return np.eye(n, k=1) + np.eye(n, k=-1)


def prolongation(coarse):
    matrix = np.zeros((2 * coarse, coarse))
    for i in range(coarse):
        matrix[2 * i, i] = 1.0
        matrix[2 * i + 1, i] += 0.5
        matrix[2 * i + 1, min(i + 1, coarse - 1)] += 0.5
    return matrix


def mode_order(n, devices):
    rows = n // devices
    if rows % 2:
        return np.arange(n)
    half = rows // 2
    low = np.arange(n // 2).reshape(devices, half)
    return np.concatenate([low, n - 1 - low], 1).reshape(-1)


def sine_matrix(n):
    index = np.arange(1, n + 1)
    return np.sqrt(2.0 / (n + 1)) * np.sin(np.pi * np.outer(index, index) / (n + 1))


def split3(x):
    high = x.astype(BF16)
    rest = x - high.astype(F32)
    mid = rest.astype(BF16)
    low = (rest - mid.astype(F32)).astype(BF16)
    return high, mid, low


def split_matrix(matrix, count):
    parts, rest = [], np.asarray(matrix, np.float64)
    for _ in range(count):
        parts.append(rest.astype(jnp.bfloat16))
        rest = rest - parts[-1].astype(np.float64)
    return jnp.asarray(np.stack(parts))


def dot6(matrix_ref, x):
    x = split3(x)
    total = None
    for left, right in ((2, 0), (0, 2), (1, 1), (1, 0), (0, 1), (0, 0)):
        term = jnp.dot(matrix_ref[left], x[right], preferred_element_type=F32)
        total = term if total is None else total + term
    return total


def dot3(parts_ref, first, weights):
    total = None
    for part in (2, 1, 0):
        term = jnp.dot(parts_ref[first + part], weights, preferred_element_type=F32)
        total = term if total is None else total + term
    return total


def restricted_rows(buf, index, start, block):
    def rows(offset):
        return buf[index + (pl.ds(PAD + 2 * start + offset, block, stride=2), slice(None))]

    return rows


def beside(parts, lanes):
    count = len(parts)
    after = [pltpu.roll(part, 1, 1) for part in parts]
    before = [pltpu.roll(part, LANES - 1, 1) for part in parts]
    sums = []
    for c in range(count):
        left = jnp.where(lanes == 0, after[c - 1] if c > 0 else 0.0, after[c])
        right = jnp.where(lanes == LANES - 1, before[c + 1] if c + 1 < count else 0.0, before[c])
        sums.append(left + right)
    return sums


def around(rows, even, row_ids, start):
    outer = rows(-2) + rows(2)
    if start == 0:
        outer = outer - jnp.where(row_ids == 0, even, 0.0)
    return outer - (even + even)


def in_plane(quad, outer, lanes):
    sums = beside(quad, lanes)
    return [(outer[c] + sums[c]) - 4.0 * quad[c] for c in range(len(quad))]


def sent_kernel(
    pot_hbm, src_hbm, end_hbm, sine_hbm,
    near_ref, far_ref, pot, src0, end, rt_ref, sine_ref,
    src, mid, parts, sem, small_sem,
):
    fine = pot_hbm.shape[1]
    coarse = fine // 2
    blocks = fine // LANES
    cut = fine // 2 + 2 * PAD
    position, devices = place()
    groups = []
    for hbm, plane, buf, index in (
        (pot_hbm, 0, pot, (0,)), (pot_hbm, 1, pot, (1,)), (src_hbm, 1, src, ()), (src_hbm, 0, src0, ()),
    ):
        for first, size in ((0, fine),):
            group = []
            for c in range(blocks):
                group.append(
                    pltpu.make_async_copy(
                        hbm.at[plane, pl.ds(first, size), pl.ds(c * LANES, LANES)],
                        buf.at[index + (c, pl.ds(PAD + first, size), slice(None))],
                        sem.at[len(groups) * blocks + c],
                    )
                )
            groups.append(group)
    for group in groups[:1]:
        for copy in group:
            copy.start()
    for group in groups[1:3]:
        for copy in group:
            copy.start()
    for copy in groups[3]:
        copy.start(priority=1)
    sine = pltpu.make_async_copy(sine_hbm, sine_ref, small_sem.at[1])
    sine.start()
    last = devices - 1
    at_end = jnp.logical_or(position == 0, position == last)
    end_copy = pltpu.make_async_copy(end_hbm.at[jnp.where(position == last, 1, 0)], end, small_sem.at[2])

    @pl.when(at_end)
    def _():
        end_copy.start()

    offset = lax.broadcasted_iota(jnp.int32, rt_ref.shape, 0) - 2 * lax.broadcasted_iota(jnp.int32, rt_ref.shape, 1)
    beside_even = jnp.where(jnp.abs(offset) == 1, 0.25, 0.0)
    rt_ref[...] = jnp.where(offset == 0, 0.5, beside_even).astype(BF16)
    edge = jnp.zeros((blocks, PAD, LANES), F32)
    for ref in (pot.at[0], pot.at[1], src, src0):
        ref[:, 0:PAD, :] = edge
        ref[:, PAD + fine : PAD + fine + PAD, :] = edge

    block = 32
    lanes = lax.broadcasted_iota(jnp.int32, (block, LANES), 1)
    row_ids = lax.broadcasted_iota(jnp.int32, (block, LANES), 0)

    def chunk(plane, start):
        where = pl.ds(start, block)
        quad, whole = [], []
        for c in range(blocks):
            rows = restricted_rows(pot, (plane, c), start, block)
            even = rows(0)
            quad.append((even + even) + (rows(1) + rows(-1)))
            if plane == 1:
                whole.append(around(rows, even, row_ids, start))
        if plane == 1:
            whole = in_plane(quad, whole, lanes)
        for c in range(blocks):
            columns = pl.ds(c * LANES, LANES)
            if plane == 0:
                mid[where, columns] = quad[c]
                pieces(0, where, columns, quad[c])
            else:
                rows = restricted_rows(src, (c,), start, block)
                even = rows(0)
                source = (even + even) + (rows(1) + rows(-1))
                value = (whole[c] + 0.25 * source) + ((quad[c] + quad[c]) + mid[where, columns])
                pieces(3, where, columns, value)

    def pieces(first, where, columns, value):
        for part, piece in enumerate(split3(value)):
            parts[first + part, where, columns] = piece

    starts = range(0, coarse, block)
    for copy in groups[0]:
        copy.wait()
    for start in starts:
        chunk(0, start)
    for group in groups[1:3]:
        for copy in group:
            copy.wait()
    for start in starts:
        chunk(1, start)
    down = 0.25 * dot3(parts, 0, rt_ref[...])
    up = 0.25 * dot3(parts, 3, rt_ref[...])
    is_even = lax.rem(position, 2) == 0
    near_ref[...] = jnp.where(is_even, up, down)
    far_ref[...] = jnp.where(is_even, down, up)
    for group in groups[3:]:
        for copy in group:
            copy.wait()
    sine.wait()

    @pl.when(at_end)
    def _():
        end_copy.wait()


def restriction_matrix(fine):
    return jnp.asarray(restriction(fine).T, BF16)


def sent_stage(devices, potential, source, end_faces):
    fine = potential.shape[1]
    coarse = fine // 2
    blocks = fine // LANES
    plane = jax.ShapeDtypeStruct((coarse, coarse), F32)
    held = (blocks, fine + 2 * PAD, LANES)
    return pl.pallas_call(
        sent_kernel,
        out_shape=(
            plane,
            plane,
            jax.ShapeDtypeStruct((2,) + held, F32),
            jax.ShapeDtypeStruct(held, F32),
            plane,
            jax.ShapeDtypeStruct((fine, coarse), BF16),
            jax.ShapeDtypeStruct((3, coarse, coarse), BF16),
        ),
        in_specs=[HBM] * 4,
        out_specs=(VMEM,) * 7,
        scratch_shapes=[
            pltpu.VMEM(held, F32),
            pltpu.VMEM((coarse, fine), F32),
            pltpu.VMEM((6, coarse, fine), BF16),
            pltpu.SemaphoreType.DMA((8 * blocks,)),
            pltpu.SemaphoreType.DMA((3,)),
        ],
        compiler_params=room(20),
        name="sent_stage",
    )(
        in_hbm(potential), in_hbm(source), in_hbm(end_faces),
        in_hbm(row_transform(coarse, devices)),
    )


def own_kernel(src0, pot, near_ref, far_ref, side_ref, end, rt_ref, sine_ref, own_ref, sent_ref, parts):
    fine, coarse = rt_ref.shape
    position, devices = place()
    last = devices - 1
    half_not_first = jnp.where(position > 0, 0.5, 0.0).astype(F32)
    block = 32
    shape = (block, LANES)
    lanes = lax.broadcasted_iota(jnp.int32, shape, 1)
    row_ids = lax.broadcasted_iota(jnp.int32, shape, 0)
    for start in range(0, coarse, block):
        where = pl.ds(start, block)
        quad, outer = [], []
        for c in range(fine // LANES):
            rows = restricted_rows(pot, (0, c), start, block)
            even = rows(0)
            quad.append((even + even) + (rows(1) + rows(-1)))
            outer.append(around(rows, even, row_ids, start))
        whole = in_plane(quad, outer, lanes)
        for c in range(fine // LANES):
            rows = restricted_rows(src0, (c,), start, block)
            even = rows(0)
            source = (even + even) + (rows(1) + rows(-1))
            value = (whole[c] + half_not_first * quad[c]) + 0.25 * source
            for part, piece in enumerate(split3(value)):
                parts[part, where, pl.ds(c * LANES, LANES)] = piece
    sent_ref[...] = dot6(sine_ref, far_ref[...])
    up = jnp.where(lax.rem(position, 2) == 0, near_ref[...], far_ref[...])
    own_ref[...] = 0.5 * dot3(parts, 0, rt_ref[...]) + up
    side = side_ref[0]
    columns = jnp.transpose(jnp.concatenate([side, side], 0))
    own_ref[0:1, :] += side[0:1]
    own_ref[coarse - 1 : coarse, :] += side[1:2]
    lanes = lax.broadcasted_iota(jnp.int32, (coarse, LANES), 1)
    own_ref[:, 0:LANES] += jnp.where(lanes == 0, columns[:, 2:3], 0.0)
    own_ref[:, coarse - LANES : coarse] += jnp.where(lanes == LANES - 1, columns[:, 3:4], 0.0)

    @pl.when(jnp.logical_or(position == 0, position == last))
    def _():
        own_ref[...] += end[...]


def own_stage(src0, pot, near, far, side_faces, end, rt, sine):
    fine, coarse = rt.shape
    return pl.pallas_call(
        own_kernel,
        out_shape=(
            jax.ShapeDtypeStruct((coarse, coarse), F32),
            jax.ShapeDtypeStruct((coarse, coarse), F32),
        ),
        in_specs=[VMEM] * 8,
        out_specs=(VMEM, VMEM),
        scratch_shapes=[pltpu.VMEM((3, coarse, fine), BF16)],
        compiler_params=room(12),
        name="own_stage",
    )(src0, pot, near, far, side_faces, end, rt, sine)


def rows_kernel(own_ref, near_ref, sine_ref, far_ref, out_ref):
    devices, _, rows, coarse = out_ref.shape
    first = dot6(sine_ref, own_ref[...] + near_ref[...])
    out_ref[:, 0] = first.reshape(devices, rows, coarse)
    out_ref[:, 1] = far_ref[...].reshape(devices, rows, coarse)


def row_transform(coarse, devices):
    return split_matrix(sine_matrix(coarse)[mode_order(coarse, devices)], 3)


def rows_stage(devices, own, near, far, sine):
    coarse = own.shape[0]
    shape = (devices, 2, coarse // devices, coarse)
    return pl.pallas_call(
        rows_kernel,
        out_shape=jax.ShapeDtypeStruct(shape, F32),
        in_specs=[VMEM] * 4,
        out_specs=VMEM,
        compiler_params=room(8),
        name="rows_stage",
    )(own, near, sine, far)


def sweep_kernel(in_ref, alpha_ref, out_ref, values, force):
    planes, _, rows, coarse = in_ref.shape
    paired = rows % 2 == 0
    sixth = 1.0 / 6.0
    shape = (rows, LANES)
    count = coarse // LANES
    lanes = lax.broadcasted_iota(jnp.int32, shape, 1)
    alpha = jnp.broadcast_to(alpha_ref[place()[0]][:, 0:1], shape)
    zero = [jnp.zeros(shape, F32)] * count
    columns = [pl.ds(c * LANES, LANES) for c in range(count)]
    for k in range(planes):
        total = in_ref[k, 0]
        if k % 2 == 0 and k > 0:
            total = total + in_ref[k - 1, 1]
        if k % 2 == 1 and k + 1 < planes:
            total = total + in_ref[k + 1, 1]
        total = total * sixth
        force[k] = total
        values[k] = total

    def held(k):
        return [values[k, :, columns[c]] for c in range(count)]

    def applied(k, under, here, over):
        sums = beside(here, lanes)
        return [
            (force[k, :, columns[c]] + alpha * here[c]) + sixth * ((under[c] + over[c]) + sums[c])
            for c in range(count)
        ]

    def step(counter, carry):
        under, here = zero, held(0)
        for k in range(planes):
            over = held(k + 1) if k + 1 < planes else zero
            for c, value in enumerate(applied(k, under, here, over)):
                values[k, :, columns[c]] = value
            under, here = here, over
        return carry

    lax.fori_loop(0, 2 * SWEEPS - 2, step, 0)

    under, here = zero, held(0)
    for k in range(planes):
        over = held(k + 1) if k + 1 < planes else zero
        black = applied(k, under, here, over)
        for c in range(count):
            mean = 0.5 * (here[c] + black[c])
            swing = 0.5 * (here[c] - black[c])
            swing = jnp.where((lanes + k) % 2 == 0, swing, -swing)
            fields = [mean + pltpu.roll(swing, rows // 2, 0)] if paired else [mean, swing]
            for f, field in enumerate(fields):
                store_solved(out_ref, planes, k, c, f * rows, field)
        under, here = here, over


def packed_sweep_kernel(in_ref, alpha_ref, out_ref, red, black, red_force, black_force):
    planes, _, rows, coarse = in_ref.shape
    slots = planes // 2
    half = rows // 2
    sixth = 1.0 / 6.0
    shape = (rows, LANES)
    count = coarse // LANES
    lanes = lax.broadcasted_iota(jnp.int32, shape, 1)
    first = lax.broadcasted_iota(jnp.int32, shape, 0) < half
    alpha = alpha_ref[place()[0]]
    zero = jnp.zeros(shape, F32)
    columns = [pl.ds(c * LANES, LANES) for c in range(count)]
    signs = [jnp.where((lanes + q) % 2 == 0, 1.0, -1.0) for q in (0, 1)]

    def forcing(k, c):
        total = in_ref[k, 0, :, columns[c]]
        if k % 2 == 0 and k > 0:
            total = total + in_ref[k - 1, 1, :, columns[c]]
        if k % 2 == 1 and k + 1 < planes:
            total = total + in_ref[k + 1, 1, :, columns[c]]
        return total

    def swapped(x):
        return pltpu.roll(x, half, 0)

    for q in range(slots):
        for c in range(count):
            one, two = forcing(q, c), forcing(q + slots, c)
            low = jnp.where(first, one, swapped(two)) * (0.5 * sixth)
            high = jnp.where(first, swapped(one), two) * (0.5 * sixth * signs[q % 2])
            red_force[q, :, columns[c]] = low + high
            black_force[q, :, columns[c]] = low - high
            red[q, :, columns[c]] = low + high

    def update(target, force, other):
        def held(q):
            return [other[q, :, columns[c]] for c in range(count)]

        here, end = held(0), held(slots - 1)
        under = [jnp.where(first, zero, swapped(x)) for x in end]
        beyond = [jnp.where(first, swapped(x), zero) for x in here]
        for q in range(slots):
            over = held(q + 1) if q + 1 < slots else beyond
            sums = beside(here, lanes)
            for c in range(count):
                target[q, :, columns[c]] = (force[q, :, columns[c]] + alpha * here[c]) + sixth * (
                    (under[c] + over[c]) + sums[c]
                )
            under, here = here, over

    update(black, black_force, red)

    def sweep(counter, carry):
        update(red, red_force, black)
        update(black, black_force, red)
        return carry

    lax.fori_loop(0, SWEEPS - 1, sweep, 0, unroll=True)

    for q in range(slots):
        for c in range(count):
            on_red, on_black = red[q, :, columns[c]], black[q, :, columns[c]]
            low = on_red + on_black
            high = signs[q % 2] * (on_red - on_black)
            store_solved(out_ref, planes, q, c, 0, jnp.where(first, low, swapped(high)))
            store_solved(out_ref, planes, q + slots, c, 0, jnp.where(first, swapped(low), high))


def store_solved(out_ref, planes, k, c, first_row, field):
    rows = field.shape[0]
    coarse = out_ref.shape[2] // 3 * 2
    where = pl.ds(first_row, rows)
    out_ref[k, where, pl.ds(c * LANES, LANES)] = field
    if k >= 2 and k % 2 == 0 or k == planes - 1:
        half = coarse // 2
        before = k - 2 if k < planes - 1 else k - 1
        side = c * LANES // half
        out_ref[before + side, where, pl.ds(coarse + c * LANES - side * half, LANES)] = field


def sweep_stage(received):
    devices, _, rows, coarse = received.shape
    packed = rows == 8 and devices % 4 == 0
    fields = 1 if rows % 2 == 0 else 2
    modes = (mode_order(coarse, devices) + 1).reshape(devices, rows)
    if packed:
        modes = np.concatenate([modes[:, : rows // 2]] * 2, 1)
    alpha = np.cos(np.pi * modes / (coarse + 1)) / 3.0
    table = jnp.asarray(np.tile(alpha[:, :, None], (1, 1, LANES)), F32)
    shape = (devices // 2 if packed else devices, rows, coarse)
    return pl.pallas_call(
        packed_sweep_kernel if packed else sweep_kernel,
        out_shape=jax.ShapeDtypeStruct((devices, fields * rows, coarse + coarse // 2), F32),
        in_specs=[VMEM, VMEM],
        out_specs=VMEM,
        scratch_shapes=[pltpu.VMEM(shape, F32)] * (4 if packed else 2),
        compiler_params=room(8 if rows % 8 == 0 else 24),
        name="sweep_stage",
    )(received, table)


def back_product(in_ref, back_ref, first, size):
    devices, held, _ = in_ref.shape
    coarse = back_ref.shape[1]
    rows = coarse // devices
    total = None
    for f in range(held // rows):
        part = in_ref[:, f * rows : (f + 1) * rows, first : first + size].reshape(coarse, size)
        high = part.astype(BF16)
        low = (part - high.astype(F32)).astype(BF16)
        for left, right in ((1, high), (0, low), (0, high)):
            term = jnp.dot(back_ref[2 * f + left], right, preferred_element_type=F32)
            total = term if total is None else total + term
    return total


def by_parity(even, odd):
    is_even = lax.rem(place()[0], 2) == 0
    pl.when(is_even)(even)
    pl.when(jnp.logical_not(is_even))(odd)


def swap_kernel(in_ref, back_ref, swap_ref):
    coarse = swap_ref.shape[0]
    half = in_ref.shape[2] - coarse

    def even():
        swap_ref[:, 0:half] = back_product(in_ref, back_ref, coarse, half)
        swap_ref[:, half:] = jnp.zeros((coarse, coarse - half), F32)

    def odd():
        swap_ref[...] = back_product(in_ref, back_ref, 0, coarse)

    by_parity(even, odd)


def back_matrices(coarse, devices, held):
    order = mode_order(coarse, devices)
    sine = sine_matrix(coarse)
    back = [sine[order].T]
    if held > coarse // devices:
        back.append(sine[coarse - 1 - order].T)
    return jnp.concatenate([split_matrix(matrix, 2) for matrix in back])


def swap_stage(coarse, received, back):
    return pl.pallas_call(
        swap_kernel,
        out_shape=jax.ShapeDtypeStruct((coarse, coarse), F32),
        in_specs=[VMEM, VMEM],
        out_specs=VMEM,
        compiler_params=room(8),
        name="swap_stage",
    )(received, back)


def add_prolonged(value, pt_ref, pot, plane, out, parts, wide, ready):
    coarse = value.shape[0]
    fine = 2 * coarse
    block = 64
    for part, piece in enumerate(split3(value)):
        parts[part] = piece
    for n in range(0, fine, coarse):
        wide[0:coarse, :] = dot3(parts, 0, pt_ref[:, n : n + coarse])
        wide[coarse : coarse + 1, :] = wide[coarse - 1 : coarse, :]
        for c in range(n // LANES, (n + coarse) // LANES):
            lanes = pl.ds(c * LANES - n, LANES)
            for start in range(0, coarse, block):
                here = wide[pl.ds(start, block), lanes]
                after = wide[pl.ds(start + 1, block), lanes]
                for odd, value in ((0, here), (1, 0.5 * (here + after))):
                    old = pot[plane, c, pl.ds(PAD + 2 * start + odd, block, stride=2), :]
                    out[c, pl.ds(2 * start + odd, block, stride=2), :] = old + value
            ready(c)


def even_kernel(in_ref, back_ref, swap_ref, pt_ref, pot, own_ref, extra_ref, out_ref, parts, wide):
    coarse, half = extra_ref.shape

    def even():
        own_ref[...] = back_product(in_ref, back_ref, 0, coarse)
        extra_ref[...] = swap_ref[:, 0:half]

    def odd():
        own_ref[...] = swap_ref[...]
        extra_ref[...] = back_product(in_ref, back_ref, coarse, half)

    by_parity(even, odd)
    add_prolonged(own_ref[...], pt_ref, pot, 0, out_ref, parts, wide, lambda c: None)


def odd_kernel(
    own_ref, swapped_ref, extra_ref, even_ref, pt_ref, pot, out_hbm, corr_hbm, out, parts, wide, sem, corr_sem
):
    stores = [
        [
            pltpu.make_async_copy(
                buf.at[c], out_hbm.at[plane, :, pl.ds(c * LANES, LANES)], sem.at[plane * out.shape[0] + c]
            )
            for c in range(out.shape[0])
        ]
        for plane, buf in ((0, even_ref), (1, out))
    ]
    for store in stores[0]:
        store.start()
    copy = pltpu.make_async_copy(own_ref, corr_hbm.at[0], corr_sem)
    copy.start()
    position, devices = place()
    own = own_ref[...]
    swapped = swapped_ref[...]
    half = extra_ref.shape[1]
    is_even = lax.rem(position, 2) == 0
    right = jnp.where(is_even, swapped[:, half:], extra_ref[...])
    above = jnp.concatenate([swapped[:, :half], right], 1)
    above = jnp.where(position == devices - 1, own, above)
    add_prolonged(
        0.5 * (own + above), pt_ref, pot, 1, out, parts, wide, lambda c: stores[1][c].start()
    )
    for store in stores[0] + stores[1]:
        store.wait()
    copy.wait()


def prolong_matrix(coarse):
    return jnp.asarray(prolongation(coarse).T, BF16)


def plane_scratch(coarse):
    return [pltpu.VMEM((3, coarse, coarse), BF16), pltpu.VMEM((coarse + PAD, coarse), F32)]


def even_stage(received, back, swap, pot):
    coarse = swap.shape[0]
    fine = 2 * coarse
    return pl.pallas_call(
        even_kernel,
        out_shape=(
            jax.ShapeDtypeStruct((coarse, coarse), F32),
            jax.ShapeDtypeStruct((coarse, received.shape[2] - coarse), F32),
            jax.ShapeDtypeStruct((fine // LANES, fine, LANES), F32),
        ),
        in_specs=[VMEM] * 5,
        out_specs=(VMEM,) * 3,
        scratch_shapes=plane_scratch(coarse),
        compiler_params=room(8),
        name="even_stage",
    )(received, back, swap, prolong_matrix(coarse), pot)


def odd_stage(own, swapped, extra, even, pot):
    coarse = own.shape[0]
    fine = 2 * coarse
    blocks = fine // LANES
    return pl.pallas_call(
        odd_kernel,
        out_shape=(
            jax.ShapeDtypeStruct((2, fine, fine), F32),
            jax.ShapeDtypeStruct((1, coarse, coarse), F32),
        ),
        in_specs=[VMEM] * 6,
        out_specs=(HBM, HBM),
        scratch_shapes=[pltpu.VMEM((blocks, fine, LANES), F32)]
        + plane_scratch(coarse)
        + [pltpu.SemaphoreType.DMA((2 * blocks,)), pltpu.SemaphoreType.DMA],
        compiler_params=room(8),
        name="odd_stage",
    )(own, swapped, extra, even, prolong_matrix(coarse), pot)


def per_device(potential, source, side_faces, end_faces):
    devices = lax.axis_size("grp") * lax.axis_size("mem")
    coarse = side_faces.shape[2]
    in_chip = [(i, i ^ 1) for i in range(devices)]
    near, far, pot, src0, end, rt, sine = sent_stage(devices, potential, source, end_faces)
    arrived = lax.ppermute(near, AXES, in_chip)
    own, far = own_stage(src0, pot, near, far, side_faces, end, rt, sine)
    sent = rows_stage(devices, own, arrived, far, sine)
    received = lax.all_to_all(sent, AXES, 0, 0, tiled=True)
    solved = sweep_stage(received)
    returned = lax.all_to_all(solved, AXES, 0, 0, tiled=True)
    back = back_matrices(coarse, devices, returned.shape[1])
    swap = swap_stage(coarse, returned, back)
    swapped = lax.ppermute(swap, AXES, in_chip)
    own, extra, even = even_stage(returned, back, swap, pot)
    return odd_stage(own, swapped, extra, even, pot)


def solution(mesh):
    split = P(AXES, None, None)
    return jax.shard_map(
        per_device,
        mesh=mesh,
        in_specs=(split, split, split, P()),
        out_specs=(split, split),
        check_vma=False,
    )
```

```python
import jax
import jax.numpy as jnp
import numpy as np
from jax import lax
from jax.experimental import pallas as pl
from jax.experimental.pallas import tpu as pltpu
from jax.sharding import PartitionSpec as P

SWEEPS = 8
AXES = ("grp", "mem")
PAD = 8
LANES = 128
F32 = jnp.float32
BF16 = jnp.bfloat16
VMEM = pl.BlockSpec(memory_space=pltpu.VMEM)
ANY = pl.BlockSpec(memory_space=pl.ANY)
HBM = pl.BlockSpec(memory_space=pltpu.HBM)


def place():
    members = lax.axis_size("mem")
    return lax.axis_index("grp") * members + lax.axis_index("mem"), lax.axis_size("grp") * members


def in_hbm(array):
    return pltpu.with_memory_space_constraint(array, pltpu.HBM)


def room(mebibytes):
    return pltpu.CompilerParams(vmem_limit_bytes=mebibytes << 20)


def restriction(fine):
    matrix = np.zeros((fine // 2, fine))
    for i in range(fine // 2):
        matrix[i, 2 * i] = 0.5
        matrix[i, 2 * i + 1] = 0.25
        if i > 0:
            matrix[i, 2 * i - 1] = 0.25
    return matrix


def neighbour_sum(n):
    return np.eye(n, k=1) + np.eye(n, k=-1)


def prolongation(coarse):
    matrix = np.zeros((2 * coarse, coarse))
    for i in range(coarse):
        matrix[2 * i, i] = 1.0
        matrix[2 * i + 1, i] += 0.5
        matrix[2 * i + 1, min(i + 1, coarse - 1)] += 0.5
    return matrix


def mode_order(n, devices):
    rows = n // devices
    if rows % 2:
        return np.arange(n)
    half = rows // 2
    low = np.arange(n // 2).reshape(devices, half)
    return np.concatenate([low, n - 1 - low], 1).reshape(-1)


def sine_matrix(n):
    index = np.arange(1, n + 1)
    return np.sqrt(2.0 / (n + 1)) * np.sin(np.pi * np.outer(index, index) / (n + 1))


def split3(x):
    high = x.astype(BF16)
    rest = x - high.astype(F32)
    mid = rest.astype(BF16)
    low = (rest - mid.astype(F32)).astype(BF16)
    return high, mid, low


def split_matrix(matrix, count):
    parts, rest = [], np.asarray(matrix, np.float64)
    for _ in range(count):
        parts.append(rest.astype(jnp.bfloat16))
        rest = rest - parts[-1].astype(np.float64)
    return jnp.asarray(np.stack(parts))


def dot6(matrix_ref, x):
    x = split3(x)
    total = None
    for left, right in ((2, 0), (0, 2), (1, 1), (1, 0), (0, 1), (0, 0)):
        term = jnp.dot(matrix_ref[left], x[right], preferred_element_type=F32)
        total = term if total is None else total + term
    return total


def dot3(parts_ref, first, weights):
    total = None
    for part in (2, 1, 0):
        term = jnp.dot(parts_ref[first + part], weights, preferred_element_type=F32)
        total = term if total is None else total + term
    return total


def restricted_rows(buf, index, start, block):
    def rows(offset):
        return buf[index + (pl.ds(PAD + 2 * start + offset, block, stride=2), slice(None))]

    return rows


def beside(parts, lanes):
    count = len(parts)
    after = [pltpu.roll(part, 1, 1) for part in parts]
    before = [pltpu.roll(part, LANES - 1, 1) for part in parts]
    sums = []
    for c in range(count):
        left = jnp.where(lanes == 0, after[c - 1] if c > 0 else 0.0, after[c])
        right = jnp.where(lanes == LANES - 1, before[c + 1] if c + 1 < count else 0.0, before[c])
        sums.append(left + right)
    return sums


def around(rows, even, row_ids, start):
    outer = rows(-2) + rows(2)
    if start == 0:
        outer = outer - jnp.where(row_ids == 0, even, 0.0)
    return outer - (even + even)


def in_plane(quad, outer, lanes):
    sums = beside(quad, lanes)
    return [(outer[c] + sums[c]) - 4.0 * quad[c] for c in range(len(quad))]


def sent_kernel(
    pot_hbm, src_hbm, end_hbm, sine_hbm,
    near_ref, far_ref, pot, src0, end, rt_ref, sine_ref,
    src, mid, parts, sem, small_sem,
):
    fine = pot_hbm.shape[1]
    coarse = fine // 2
    blocks = fine // LANES
    cut = fine // 2 + 2 * PAD
    position, devices = place()
    groups = []
    for hbm, plane, buf, index in (
        (pot_hbm, 0, pot, (0,)), (pot_hbm, 1, pot, (1,)), (src_hbm, 1, src, ()), (src_hbm, 0, src0, ()),
    ):
        for first, size in ((0, fine),):
            group = []
            for c in range(blocks):
                group.append(
                    pltpu.make_async_copy(
                        hbm.at[plane, pl.ds(first, size), pl.ds(c * LANES, LANES)],
                        buf.at[index + (c, pl.ds(PAD + first, size), slice(None))],
                        sem.at[len(groups) * blocks + c],
                    )
                )
            groups.append(group)
    for group in groups[:1]:
        for copy in group:
            copy.start()
    for group in groups[1:3]:
        for copy in group:
            copy.start()
    for copy in groups[3]:
        copy.start(priority=1)
    sine = pltpu.make_async_copy(sine_hbm, sine_ref, small_sem.at[1])
    sine.start(priority=1)
    last = devices - 1
    at_end = jnp.logical_or(position == 0, position == last)
    end_copy = pltpu.make_async_copy(end_hbm.at[jnp.where(position == last, 1, 0)], end, small_sem.at[2])

    @pl.when(at_end)
    def _():
        end_copy.start()

    offset = lax.broadcasted_iota(jnp.int32, rt_ref.shape, 0) - 2 * lax.broadcasted_iota(jnp.int32, rt_ref.shape, 1)
    beside_even = jnp.where(jnp.abs(offset) == 1, 0.25, 0.0)
    rt_ref[...] = jnp.where(offset == 0, 0.5, beside_even).astype(BF16)
    edge = jnp.zeros((blocks, PAD, LANES), F32)
    for ref in (pot.at[0], pot.at[1], src, src0):
        ref[:, 0:PAD, :] = edge
        ref[:, PAD + fine : PAD + fine + PAD, :] = edge

    block = 32
    lanes = lax.broadcasted_iota(jnp.int32, (block, LANES), 1)
    row_ids = lax.broadcasted_iota(jnp.int32, (block, LANES), 0)

    def chunk(plane, start):
        where = pl.ds(start, block)
        quad, whole = [], []
        for c in range(blocks):
            rows = restricted_rows(pot, (plane, c), start, block)
            even = rows(0)
            quad.append((even + even) + (rows(1) + rows(-1)))
            if plane == 1:
                whole.append(around(rows, even, row_ids, start))
        if plane == 1:
            whole = in_plane(quad, whole, lanes)
        for c in range(blocks):
            columns = pl.ds(c * LANES, LANES)
            if plane == 0:
                mid[where, columns] = quad[c]
                pieces(0, where, columns, quad[c])
            else:
                rows = restricted_rows(src, (c,), start, block)
                even = rows(0)
                source = (even + even) + (rows(1) + rows(-1))
                value = (whole[c] + 0.25 * source) + ((quad[c] + quad[c]) + mid[where, columns])
                pieces(3, where, columns, value)

    def pieces(first, where, columns, value):
        for part, piece in enumerate(split3(value)):
            parts[first + part, where, columns] = piece

    starts = range(0, coarse, block)
    for copy in groups[0]:
        copy.wait()
    for start in starts:
        chunk(0, start)
    for group in groups[1:3]:
        for copy in group:
            copy.wait()
    for start in starts:
        chunk(1, start)
    down = 0.25 * dot3(parts, 0, rt_ref[...])
    up = 0.25 * dot3(parts, 3, rt_ref[...])
    is_even = lax.rem(position, 2) == 0
    near_ref[...] = jnp.where(is_even, up, down)
    far_ref[...] = jnp.where(is_even, down, up)
    for group in groups[3:]:
        for copy in group:
            copy.wait()
    sine.wait()

    @pl.when(at_end)
    def _():
        end_copy.wait()


def restriction_matrix(fine):
    return jnp.asarray(restriction(fine).T, BF16)


def sent_stage(devices, potential, source, end_faces):
    fine = potential.shape[1]
    coarse = fine // 2
    blocks = fine // LANES
    plane = jax.ShapeDtypeStruct((coarse, coarse), F32)
    held = (blocks, fine + 2 * PAD, LANES)
    return pl.pallas_call(
        sent_kernel,
        out_shape=(
            plane,
            plane,
            jax.ShapeDtypeStruct((2,) + held, F32),
            jax.ShapeDtypeStruct(held, F32),
            plane,
            jax.ShapeDtypeStruct((fine, coarse), BF16),
            jax.ShapeDtypeStruct((3, coarse, coarse), BF16),
        ),
        in_specs=[HBM] * 4,
        out_specs=(VMEM,) * 7,
        scratch_shapes=[
            pltpu.VMEM(held, F32),
            pltpu.VMEM((coarse, fine), F32),
            pltpu.VMEM((6, coarse, fine), BF16),
            pltpu.SemaphoreType.DMA((8 * blocks,)),
            pltpu.SemaphoreType.DMA((3,)),
        ],
        compiler_params=room(20),
        name="sent_stage",
    )(
        in_hbm(potential), in_hbm(source), in_hbm(end_faces),
        in_hbm(row_transform(coarse, devices)),
    )


def own_kernel(src0, pot, near_ref, far_ref, side_ref, end, rt_ref, sine_ref, own_ref, sent_ref, parts):
    fine, coarse = rt_ref.shape
    position, devices = place()
    last = devices - 1
    half_not_first = jnp.where(position > 0, 0.5, 0.0).astype(F32)
    block = 32
    shape = (block, LANES)
    lanes = lax.broadcasted_iota(jnp.int32, shape, 1)
    row_ids = lax.broadcasted_iota(jnp.int32, shape, 0)
    for start in range(0, coarse, block):
        where = pl.ds(start, block)
        quad, outer = [], []
        for c in range(fine // LANES):
            rows = restricted_rows(pot, (0, c), start, block)
            even = rows(0)
            quad.append((even + even) + (rows(1) + rows(-1)))
            outer.append(around(rows, even, row_ids, start))
        whole = in_plane(quad, outer, lanes)
        for c in range(fine // LANES):
            rows = restricted_rows(src0, (c,), start, block)
            even = rows(0)
            source = (even + even) + (rows(1) + rows(-1))
            value = (whole[c] + half_not_first * quad[c]) + 0.25 * source
            for part, piece in enumerate(split3(value)):
                parts[part, where, pl.ds(c * LANES, LANES)] = piece
    sent_ref[...] = dot6(sine_ref, far_ref[...])
    up = jnp.where(lax.rem(position, 2) == 0, near_ref[...], far_ref[...])
    own_ref[...] = 0.5 * dot3(parts, 0, rt_ref[...]) + up
    side = side_ref[0]
    columns = jnp.transpose(jnp.concatenate([side, side], 0))
    own_ref[0:1, :] += side[0:1]
    own_ref[coarse - 1 : coarse, :] += side[1:2]
    lanes = lax.broadcasted_iota(jnp.int32, (coarse, LANES), 1)
    own_ref[:, 0:LANES] += jnp.where(lanes == 0, columns[:, 2:3], 0.0)
    own_ref[:, coarse - LANES : coarse] += jnp.where(lanes == LANES - 1, columns[:, 3:4], 0.0)

    @pl.when(jnp.logical_or(position == 0, position == last))
    def _():
        own_ref[...] += end[...]


def own_stage(src0, pot, near, far, side_faces, end, rt, sine):
    fine, coarse = rt.shape
    return pl.pallas_call(
        own_kernel,
        out_shape=(
            jax.ShapeDtypeStruct((coarse, coarse), F32),
            jax.ShapeDtypeStruct((coarse, coarse), F32),
        ),
        in_specs=[VMEM] * 8,
        out_specs=(VMEM, VMEM),
        scratch_shapes=[pltpu.VMEM((3, coarse, fine), BF16)],
        compiler_params=room(12),
        name="own_stage",
    )(src0, pot, near, far, side_faces, end, rt, sine)


def rows_kernel(own_ref, near_ref, sine_ref, far_ref, out_ref):
    devices, _, rows, coarse = out_ref.shape
    first = dot6(sine_ref, own_ref[...] + near_ref[...])
    out_ref[:, 0] = first.reshape(devices, rows, coarse)
    out_ref[:, 1] = far_ref[...].reshape(devices, rows, coarse)


def row_transform(coarse, devices):
    return split_matrix(sine_matrix(coarse)[mode_order(coarse, devices)], 3)


def rows_stage(devices, own, near, far, sine):
    coarse = own.shape[0]
    shape = (devices, 2, coarse // devices, coarse)
    return pl.pallas_call(
        rows_kernel,
        out_shape=jax.ShapeDtypeStruct(shape, F32),
        in_specs=[VMEM] * 4,
        out_specs=VMEM,
        compiler_params=room(8),
        name="rows_stage",
    )(own, near, sine, far)


def sweep_kernel(in_ref, alpha_ref, out_ref, values, force):
    planes, _, rows, coarse = in_ref.shape
    paired = rows % 2 == 0
    sixth = 1.0 / 6.0
    shape = (rows, LANES)
    count = coarse // LANES
    lanes = lax.broadcasted_iota(jnp.int32, shape, 1)
    alpha = jnp.broadcast_to(alpha_ref[place()[0]][:, 0:1], shape)
    zero = [jnp.zeros(shape, F32)] * count
    columns = [pl.ds(c * LANES, LANES) for c in range(count)]
    for k in range(planes):
        total = in_ref[k, 0]
        if k % 2 == 0 and k > 0:
            total = total + in_ref[k - 1, 1]
        if k % 2 == 1 and k + 1 < planes:
            total = total + in_ref[k + 1, 1]
        total = total * sixth
        force[k] = total
        values[k] = total

    def held(k):
        return [values[k, :, columns[c]] for c in range(count)]

    def applied(k, under, here, over):
        sums = beside(here, lanes)
        return [
            (force[k, :, columns[c]] + alpha * here[c]) + sixth * ((under[c] + over[c]) + sums[c])
            for c in range(count)
        ]

    def step(counter, carry):
        under, here = zero, held(0)
        for k in range(planes):
            over = held(k + 1) if k + 1 < planes else zero
            for c, value in enumerate(applied(k, under, here, over)):
                values[k, :, columns[c]] = value
            under, here = here, over
        return carry

    lax.fori_loop(0, 2 * SWEEPS - 2, step, 0)

    under, here = zero, held(0)
    for k in range(planes):
        over = held(k + 1) if k + 1 < planes else zero
        black = applied(k, under, here, over)
        for c in range(count):
            mean = 0.5 * (here[c] + black[c])
            swing = 0.5 * (here[c] - black[c])
            swing = jnp.where((lanes + k) % 2 == 0, swing, -swing)
            fields = [mean + pltpu.roll(swing, rows // 2, 0)] if paired else [mean, swing]
            for f, field in enumerate(fields):
                store_solved(out_ref, planes, k, c, f * rows, field)
        under, here = here, over


def packed_sweep_kernel(in_ref, alpha_ref, out_ref, red, black, red_force, black_force):
    planes, _, rows, coarse = in_ref.shape
    slots = planes // 2
    half = rows // 2
    sixth = 1.0 / 6.0
    shape = (rows, LANES)
    count = coarse // LANES
    lanes = lax.broadcasted_iota(jnp.int32, shape, 1)
    first = lax.broadcasted_iota(jnp.int32, shape, 0) < half
    alpha = alpha_ref[place()[0]]
    zero = jnp.zeros(shape, F32)
    columns = [pl.ds(c * LANES, LANES) for c in range(count)]
    signs = [jnp.where((lanes + q) % 2 == 0, 1.0, -1.0) for q in (0, 1)]

    def forcing(k, c):
        total = in_ref[k, 0, :, columns[c]]
        if k % 2 == 0 and k > 0:
            total = total + in_ref[k - 1, 1, :, columns[c]]
        if k % 2 == 1 and k + 1 < planes:
            total = total + in_ref[k + 1, 1, :, columns[c]]
        return total

    def swapped(x):
        return pltpu.roll(x, half, 0)

    for q in range(slots):
        for c in range(count):
            one, two = forcing(q, c), forcing(q + slots, c)
            low = jnp.where(first, one, swapped(two)) * (0.5 * sixth)
            high = jnp.where(first, swapped(one), two) * (0.5 * sixth * signs[q % 2])
            red_force[q, :, columns[c]] = low + high
            black_force[q, :, columns[c]] = low - high
            red[q, :, columns[c]] = low + high

    def update(target, force, other):
        def held(q):
            return [other[q, :, columns[c]] for c in range(count)]

        here, end = held(0), held(slots - 1)
        under = [jnp.where(first, zero, swapped(x)) for x in end]
        beyond = [jnp.where(first, swapped(x), zero) for x in here]
        for q in range(slots):
            over = held(q + 1) if q + 1 < slots else beyond
            sums = beside(here, lanes)
            for c in range(count):
                target[q, :, columns[c]] = (force[q, :, columns[c]] + alpha * here[c]) + sixth * (
                    (under[c] + over[c]) + sums[c]
                )
            under, here = here, over

    update(black, black_force, red)

    def sweep(counter, carry):
        update(red, red_force, black)
        update(black, black_force, red)
        return carry

    lax.fori_loop(0, SWEEPS - 1, sweep, 0, unroll=True)

    for q in range(slots):
        for c in range(count):
            on_red, on_black = red[q, :, columns[c]], black[q, :, columns[c]]
            low = on_red + on_black
            high = signs[q % 2] * (on_red - on_black)
            store_solved(out_ref, planes, q, c, 0, jnp.where(first, low, swapped(high)))
            store_solved(out_ref, planes, q + slots, c, 0, jnp.where(first, swapped(low), high))


def store_solved(out_ref, planes, k, c, first_row, field):
    rows = field.shape[0]
    coarse = out_ref.shape[2] // 3 * 2
    where = pl.ds(first_row, rows)
    out_ref[k, where, pl.ds(c * LANES, LANES)] = field
    if k >= 2 and k % 2 == 0 or k == planes - 1:
        half = coarse // 2
        before = k - 2 if k < planes - 1 else k - 1
        side = c * LANES // half
        out_ref[before + side, where, pl.ds(coarse + c * LANES - side * half, LANES)] = field


def sweep_stage(received):
    devices, _, rows, coarse = received.shape
    packed = rows == 8 and devices % 4 == 0
    fields = 1 if rows % 2 == 0 else 2
    modes = (mode_order(coarse, devices) + 1).reshape(devices, rows)
    if packed:
        modes = np.concatenate([modes[:, : rows // 2]] * 2, 1)
    alpha = np.cos(np.pi * modes / (coarse + 1)) / 3.0
    table = jnp.asarray(np.tile(alpha[:, :, None], (1, 1, LANES)), F32)
    shape = (devices // 2 if packed else devices, rows, coarse)
    return pl.pallas_call(
        packed_sweep_kernel if packed else sweep_kernel,
        out_shape=jax.ShapeDtypeStruct((devices, fields * rows, coarse + coarse // 2), F32),
        in_specs=[VMEM, VMEM],
        out_specs=VMEM,
        scratch_shapes=[pltpu.VMEM(shape, F32)] * (4 if packed else 2),
        compiler_params=room(8 if rows % 8 == 0 else 24),
        name="sweep_stage",
    )(received, table)


def back_product(in_ref, back_ref, first, size):
    devices, held, _ = in_ref.shape
    coarse = back_ref.shape[1]
    rows = coarse // devices
    total = None
    for f in range(held // rows):
        part = in_ref[:, f * rows : (f + 1) * rows, first : first + size].reshape(coarse, size)
        term = dot6(back_ref.at[pl.ds(3 * f, 3)], part)
        total = term if total is None else total + term
    return total


def by_parity(even, odd):
    is_even = lax.rem(place()[0], 2) == 0
    pl.when(is_even)(even)
    pl.when(jnp.logical_not(is_even))(odd)


def swap_kernel(in_ref, back_ref, swap_ref):
    coarse = swap_ref.shape[0]
    half = in_ref.shape[2] - coarse

    def even():
        swap_ref[:, 0:half] = back_product(in_ref, back_ref, coarse, half)
        swap_ref[:, half:] = jnp.zeros((coarse, coarse - half), F32)

    def odd():
        swap_ref[...] = back_product(in_ref, back_ref, 0, coarse)

    by_parity(even, odd)


def back_matrices(coarse, devices, held):
    order = mode_order(coarse, devices)
    sine = sine_matrix(coarse)
    back = [sine[order].T]
    if held > coarse // devices:
        back.append(sine[coarse - 1 - order].T)
    return jnp.concatenate([split_matrix(matrix, 3) for matrix in back])


def swap_stage(coarse, received, back):
    return pl.pallas_call(
        swap_kernel,
        out_shape=jax.ShapeDtypeStruct((coarse, coarse), F32),
        in_specs=[VMEM, VMEM],
        out_specs=VMEM,
        compiler_params=room(16),
        name="swap_stage",
    )(received, back)


def add_prolonged(value, pt_ref, pot, plane, out, parts, wide, ready):
    coarse = value.shape[0]
    fine = 2 * coarse
    block = 64
    for part, piece in enumerate(split3(value)):
        parts[part] = piece
    for n in range(0, fine, coarse):
        wide[0:coarse, :] = dot3(parts, 0, pt_ref[:, n : n + coarse])
        wide[coarse : coarse + 1, :] = wide[coarse - 1 : coarse, :]
        for c in range(n // LANES, (n + coarse) // LANES):
            lanes = pl.ds(c * LANES - n, LANES)
            for start in range(0, coarse, block):
                here = wide[pl.ds(start, block), lanes]
                after = wide[pl.ds(start + 1, block), lanes]
                for odd, value in ((0, here), (1, 0.5 * (here + after))):
                    old = pot[plane, c, pl.ds(PAD + 2 * start + odd, block, stride=2), :]
                    out[c, pl.ds(2 * start + odd, block, stride=2), :] = old + value
            ready(c)


def even_kernel(in_ref, back_ref, swap_ref, pt_ref, pot, own_ref, extra_ref, out_ref, parts, wide):
    coarse, half = extra_ref.shape

    def even():
        own_ref[...] = back_product(in_ref, back_ref, 0, coarse)
        extra_ref[...] = swap_ref[:, 0:half]

    def odd():
        own_ref[...] = swap_ref[...]
        extra_ref[...] = back_product(in_ref, back_ref, coarse, half)

    by_parity(even, odd)
    add_prolonged(own_ref[...], pt_ref, pot, 0, out_ref, parts, wide, lambda c: None)


def odd_kernel(
    own_ref, swapped_ref, extra_ref, even_ref, pt_ref, pot, out_hbm, corr_hbm, out, parts, wide, sem, corr_sem
):
    stores = [
        [
            pltpu.make_async_copy(
                buf.at[c], out_hbm.at[plane, :, pl.ds(c * LANES, LANES)], sem.at[plane * out.shape[0] + c]
            )
            for c in range(out.shape[0])
        ]
        for plane, buf in ((0, even_ref), (1, out))
    ]
    for store in stores[0]:
        store.start()
    copy = pltpu.make_async_copy(own_ref, corr_hbm.at[0], corr_sem)
    copy.start()
    position, devices = place()
    own = own_ref[...]
    swapped = swapped_ref[...]
    half = extra_ref.shape[1]
    is_even = lax.rem(position, 2) == 0
    right = jnp.where(is_even, swapped[:, half:], extra_ref[...])
    above = jnp.concatenate([swapped[:, :half], right], 1)
    above = jnp.where(position == devices - 1, own, above)
    add_prolonged(
        0.5 * (own + above), pt_ref, pot, 1, out, parts, wide, lambda c: stores[1][c].start()
    )
    for store in stores[0] + stores[1]:
        store.wait()
    copy.wait()


def prolong_matrix(coarse):
    return jnp.asarray(prolongation(coarse).T, BF16)


def plane_scratch(coarse):
    return [pltpu.VMEM((3, coarse, coarse), BF16), pltpu.VMEM((coarse + PAD, coarse), F32)]


def even_stage(received, back, swap, pot):
    coarse = swap.shape[0]
    fine = 2 * coarse
    return pl.pallas_call(
        even_kernel,
        out_shape=(
            jax.ShapeDtypeStruct((coarse, coarse), F32),
            jax.ShapeDtypeStruct((coarse, received.shape[2] - coarse), F32),
            jax.ShapeDtypeStruct((fine // LANES, fine, LANES), F32),
        ),
        in_specs=[VMEM] * 5,
        out_specs=(VMEM,) * 3,
        scratch_shapes=plane_scratch(coarse),
        compiler_params=room(16),
        name="even_stage",
    )(received, back, swap, prolong_matrix(coarse), pot)


def odd_stage(own, swapped, extra, even, pot):
    coarse = own.shape[0]
    fine = 2 * coarse
    blocks = fine // LANES
    return pl.pallas_call(
        odd_kernel,
        out_shape=(
            jax.ShapeDtypeStruct((2, fine, fine), F32),
            jax.ShapeDtypeStruct((1, coarse, coarse), F32),
        ),
        in_specs=[VMEM] * 6,
        out_specs=(HBM, HBM),
        scratch_shapes=[pltpu.VMEM((blocks, fine, LANES), F32)]
        + plane_scratch(coarse)
        + [pltpu.SemaphoreType.DMA((2 * blocks,)), pltpu.SemaphoreType.DMA],
        compiler_params=room(8),
        name="odd_stage",
    )(own, swapped, extra, even, prolong_matrix(coarse), pot)


def per_device(potential, source, side_faces, end_faces):
    devices = lax.axis_size("grp") * lax.axis_size("mem")
    coarse = side_faces.shape[2]
    in_chip = [(i, i ^ 1) for i in range(devices)]
    near, far, pot, src0, end, rt, sine = sent_stage(devices, potential, source, end_faces)
    arrived = lax.ppermute(near, AXES, in_chip)
    own, far = own_stage(src0, pot, near, far, side_faces, end, rt, sine)
    sent = rows_stage(devices, own, arrived, far, sine)
    received = lax.all_to_all(sent, AXES, 0, 0, tiled=True)
    solved = sweep_stage(received)
    returned = lax.all_to_all(solved, AXES, 0, 0, tiled=True)
    back = back_matrices(coarse, devices, returned.shape[1])
    swap = swap_stage(coarse, returned, back)
    swapped = lax.ppermute(swap, AXES, in_chip)
    own, extra, even = even_stage(returned, back, swap, pot)
    return odd_stage(own, swapped, extra, even, pot)


def solution(mesh):
    split = P(AXES, None, None)
    return jax.shard_map(
        per_device,
        mesh=mesh,
        in_specs=(split, split, split, P()),
        out_specs=(split, split),
        check_vma=False,
    )
```

```python
import jax
import jax.numpy as jnp
import numpy as np
from jax import lax
from jax.experimental import pallas as pl
from jax.experimental.pallas import tpu as pltpu
from jax.sharding import PartitionSpec as P

SWEEPS = 8
AXES = ("grp", "mem")
PAD = 8
LANES = 128
F32 = jnp.float32
BF16 = jnp.bfloat16
VMEM = pl.BlockSpec(memory_space=pltpu.VMEM)
ANY = pl.BlockSpec(memory_space=pl.ANY)
HBM = pl.BlockSpec(memory_space=pltpu.HBM)


def place():
    members = lax.axis_size("mem")
    return lax.axis_index("grp") * members + lax.axis_index("mem"), lax.axis_size("grp") * members


def in_hbm(array):
    return pltpu.with_memory_space_constraint(array, pltpu.HBM)


def room(mebibytes):
    return pltpu.CompilerParams(vmem_limit_bytes=mebibytes << 20)


def restriction(fine):
    matrix = np.zeros((fine // 2, fine))
    for i in range(fine // 2):
        matrix[i, 2 * i] = 0.5
        matrix[i, 2 * i + 1] = 0.25
        if i > 0:
            matrix[i, 2 * i - 1] = 0.25
    return matrix


def neighbour_sum(n):
    return np.eye(n, k=1) + np.eye(n, k=-1)


def prolongation(coarse):
    matrix = np.zeros((2 * coarse, coarse))
    for i in range(coarse):
        matrix[2 * i, i] = 1.0
        matrix[2 * i + 1, i] += 0.5
        matrix[2 * i + 1, min(i + 1, coarse - 1)] += 0.5
    return matrix


def column_order(coarse):
    columns = np.arange(coarse)
    return np.concatenate([columns[0::2], columns[1::2]]) if coarse == 2 * LANES else columns


def ordering(coarse, back):
    held = lax.broadcasted_iota(jnp.int32, (coarse, coarse), 0 if back else 1)
    natural = lax.broadcasted_iota(jnp.int32, (coarse, coarse), 1 if back else 0)
    if coarse == 2 * LANES:
        held = jnp.where(held < LANES, 2 * held, 2 * (held - LANES) + 1)
    return jnp.where(held == natural, 1.0, 0.0).astype(BF16)


def dot_exact(x, weights):
    total = None
    for part in reversed(split3(x)):
        term = jnp.dot(part, weights, preferred_element_type=F32)
        total = term if total is None else total + term
    return total


def mode_order(n, devices):
    rows = n // devices
    if rows % 2:
        return np.arange(n)
    half = rows // 2
    low = np.arange(n // 2).reshape(devices, half)
    return np.concatenate([low, n - 1 - low], 1).reshape(-1)


def sine_matrix(n):
    index = np.arange(1, n + 1)
    return np.sqrt(2.0 / (n + 1)) * np.sin(np.pi * np.outer(index, index) / (n + 1))


def split3(x):
    high = x.astype(BF16)
    rest = x - high.astype(F32)
    mid = rest.astype(BF16)
    low = (rest - mid.astype(F32)).astype(BF16)
    return high, mid, low


def split_matrix(matrix, count):
    parts, rest = [], np.asarray(matrix, np.float64)
    for _ in range(count):
        parts.append(rest.astype(jnp.bfloat16))
        rest = rest - parts[-1].astype(np.float64)
    return jnp.asarray(np.stack(parts))


def dot6(matrix_ref, x):
    x = split3(x)
    total = None
    for left, right in ((2, 0), (0, 2), (1, 1), (1, 0), (0, 1), (0, 0)):
        term = jnp.dot(matrix_ref[left], x[right], preferred_element_type=F32)
        total = term if total is None else total + term
    return total


def dot3(parts_ref, first, weights):
    total = None
    for part in (2, 1, 0):
        term = jnp.dot(parts_ref[first + part], weights, preferred_element_type=F32)
        total = term if total is None else total + term
    return total


def restricted_rows(buf, index, start, block):
    def rows(offset):
        return buf[index + (pl.ds(PAD + 2 * start + offset, block, stride=2), slice(None))]

    return rows


def beside(parts, lanes):
    count = len(parts)
    after = [pltpu.roll(part, 1, 1) for part in parts]
    before = [pltpu.roll(part, LANES - 1, 1) for part in parts]
    sums = []
    for c in range(count):
        left = jnp.where(lanes == 0, after[c - 1] if c > 0 else 0.0, after[c])
        right = jnp.where(lanes == LANES - 1, before[c + 1] if c + 1 < count else 0.0, before[c])
        sums.append(left + right)
    return sums


def around(rows, even, row_ids, start):
    outer = rows(-2) + rows(2)
    if start == 0:
        outer = outer - jnp.where(row_ids == 0, even, 0.0)
    return outer - (even + even)


def in_plane(quad, outer, lanes):
    sums = beside(quad, lanes)
    return [(outer[c] + sums[c]) - 4.0 * quad[c] for c in range(len(quad))]


def beside_columns(parts, lanes):
    if len(parts) != 2:
        return beside(parts, lanes)
    even, odd = parts
    return [
        odd + jnp.where(lanes == 0, 0.0, pltpu.roll(odd, 1, 1)),
        even + jnp.where(lanes == LANES - 1, 0.0, pltpu.roll(even, LANES - 1, 1)),
    ]


def column_sign(lanes, count, k, c):
    if count == 2:
        return jnp.full(lanes.shape, 1.0 if (k + c) % 2 == 0 else -1.0, F32)
    return jnp.where((lanes + k) % 2 == 0, 1.0, -1.0)


def sent_kernel(
    pot_hbm, src_hbm, end_hbm, sine_hbm,
    near_ref, far_ref, pot, src0, end, rt_ref, sine_ref,
    src, mid, parts, sem, small_sem,
):
    fine = pot_hbm.shape[1]
    coarse = fine // 2
    blocks = fine // LANES
    cut = fine // 2 + 2 * PAD
    position, devices = place()
    groups = []
    for hbm, plane, buf, index in (
        (pot_hbm, 0, pot, (0,)), (pot_hbm, 1, pot, (1,)), (src_hbm, 1, src, ()), (src_hbm, 0, src0, ()),
    ):
        for first, size in ((0, fine),):
            group = []
            for c in range(blocks):
                group.append(
                    pltpu.make_async_copy(
                        hbm.at[plane, pl.ds(first, size), pl.ds(c * LANES, LANES)],
                        buf.at[index + (c, pl.ds(PAD + first, size), slice(None))],
                        sem.at[len(groups) * blocks + c],
                    )
                )
            groups.append(group)
    for group in groups[:1]:
        for copy in group:
            copy.start()
    for group in groups[1:3]:
        for copy in group:
            copy.start()
    for copy in groups[3]:
        copy.start(priority=1)
    sine = pltpu.make_async_copy(sine_hbm, sine_ref, small_sem.at[1])
    sine.start(priority=1)
    last = devices - 1
    at_end = jnp.logical_or(position == 0, position == last)
    end_copy = pltpu.make_async_copy(end_hbm.at[jnp.where(position == last, 1, 0)], end, small_sem.at[2])

    @pl.when(at_end)
    def _():
        end_copy.start()

    target = lax.broadcasted_iota(jnp.int32, rt_ref.shape, 1)
    if coarse == 2 * LANES:
        target = jnp.where(target < LANES, 2 * target, 2 * (target - LANES) + 1)
    offset = lax.broadcasted_iota(jnp.int32, rt_ref.shape, 0) - 2 * target
    beside_even = jnp.where(jnp.abs(offset) == 1, 0.25, 0.0)
    rt_ref[...] = jnp.where(offset == 0, 0.5, beside_even).astype(BF16)
    edge = jnp.zeros((blocks, PAD, LANES), F32)
    for ref in (pot.at[0], pot.at[1], src, src0):
        ref[:, 0:PAD, :] = edge
        ref[:, PAD + fine : PAD + fine + PAD, :] = edge

    block = 32
    lanes = lax.broadcasted_iota(jnp.int32, (block, LANES), 1)
    row_ids = lax.broadcasted_iota(jnp.int32, (block, LANES), 0)

    def chunk(plane, start):
        where = pl.ds(start, block)
        quad, whole = [], []
        for c in range(blocks):
            rows = restricted_rows(pot, (plane, c), start, block)
            even = rows(0)
            quad.append((even + even) + (rows(1) + rows(-1)))
            if plane == 1:
                whole.append(around(rows, even, row_ids, start))
        if plane == 1:
            whole = in_plane(quad, whole, lanes)
        for c in range(blocks):
            columns = pl.ds(c * LANES, LANES)
            if plane == 0:
                mid[where, columns] = quad[c]
                pieces(0, where, columns, quad[c])
            else:
                rows = restricted_rows(src, (c,), start, block)
                even = rows(0)
                source = (even + even) + (rows(1) + rows(-1))
                value = (whole[c] + 0.25 * source) + ((quad[c] + quad[c]) + mid[where, columns])
                pieces(3, where, columns, value)

    def pieces(first, where, columns, value):
        for part, piece in enumerate(split3(value)):
            parts[first + part, where, columns] = piece

    starts = range(0, coarse, block)
    for copy in groups[0]:
        copy.wait()
    for start in starts:
        chunk(0, start)
    for group in groups[1:3]:
        for copy in group:
            copy.wait()
    for start in starts:
        chunk(1, start)
    down = 0.25 * dot3(parts, 0, rt_ref[...])
    up = 0.25 * dot3(parts, 3, rt_ref[...])
    is_even = lax.rem(position, 2) == 0
    near_ref[...] = jnp.where(is_even, up, down)
    far_ref[...] = jnp.where(is_even, down, up)
    for group in groups[3:]:
        for copy in group:
            copy.wait()
    sine.wait()

    @pl.when(at_end)
    def _():
        end_copy.wait()


def restriction_matrix(fine):
    return jnp.asarray(restriction(fine).T, BF16)


def sent_stage(devices, potential, source, end_faces):
    fine = potential.shape[1]
    coarse = fine // 2
    blocks = fine // LANES
    plane = jax.ShapeDtypeStruct((coarse, coarse), F32)
    held = (blocks, fine + 2 * PAD, LANES)
    return pl.pallas_call(
        sent_kernel,
        out_shape=(
            plane,
            plane,
            jax.ShapeDtypeStruct((2,) + held, F32),
            jax.ShapeDtypeStruct(held, F32),
            plane,
            jax.ShapeDtypeStruct((fine, coarse), BF16),
            jax.ShapeDtypeStruct((3, coarse, coarse), BF16),
        ),
        in_specs=[HBM] * 4,
        out_specs=(VMEM,) * 7,
        scratch_shapes=[
            pltpu.VMEM(held, F32),
            pltpu.VMEM((coarse, fine), F32),
            pltpu.VMEM((6, coarse, fine), BF16),
            pltpu.SemaphoreType.DMA((8 * blocks,)),
            pltpu.SemaphoreType.DMA((3,)),
        ],
        compiler_params=room(20),
        name="sent_stage",
    )(
        in_hbm(potential), in_hbm(source), in_hbm(end_faces),
        in_hbm(row_transform(coarse, devices)),
    )


def own_kernel(src0, pot, near_ref, far_ref, side_ref, end, rt_ref, sine_ref, own_ref, sent_ref, parts):
    fine, coarse = rt_ref.shape
    position, devices = place()
    last = devices - 1
    half_not_first = jnp.where(position > 0, 0.5, 0.0).astype(F32)
    block = 32
    shape = (block, LANES)
    lanes = lax.broadcasted_iota(jnp.int32, shape, 1)
    row_ids = lax.broadcasted_iota(jnp.int32, shape, 0)
    for start in range(0, coarse, block):
        where = pl.ds(start, block)
        quad, outer = [], []
        for c in range(fine // LANES):
            rows = restricted_rows(pot, (0, c), start, block)
            even = rows(0)
            quad.append((even + even) + (rows(1) + rows(-1)))
            outer.append(around(rows, even, row_ids, start))
        whole = in_plane(quad, outer, lanes)
        for c in range(fine // LANES):
            rows = restricted_rows(src0, (c,), start, block)
            even = rows(0)
            source = (even + even) + (rows(1) + rows(-1))
            value = (whole[c] + half_not_first * quad[c]) + 0.25 * source
            for part, piece in enumerate(split3(value)):
                parts[part, where, pl.ds(c * LANES, LANES)] = piece
    sent_ref[...] = dot6(sine_ref, far_ref[...])
    up = jnp.where(lax.rem(position, 2) == 0, near_ref[...], far_ref[...])
    own_ref[...] = 0.5 * dot3(parts, 0, rt_ref[...]) + up
    side = side_ref[0]
    columns = jnp.transpose(jnp.concatenate([side, side], 0))
    order = ordering(coarse, False)
    ends = dot_exact(jnp.concatenate([side, side], 0), order)
    own_ref[0:1, :] += ends[0:1]
    own_ref[coarse - 1 : coarse, :] += ends[1:2]
    lanes = lax.broadcasted_iota(jnp.int32, (coarse, LANES), 1)
    own_ref[:, 0:LANES] += jnp.where(lanes == 0, columns[:, 2:3], 0.0)
    own_ref[:, coarse - LANES : coarse] += jnp.where(lanes == LANES - 1, columns[:, 3:4], 0.0)

    @pl.when(jnp.logical_or(position == 0, position == last))
    def _():
        own_ref[...] += dot_exact(end[...], order)


def own_stage(src0, pot, near, far, side_faces, end, rt, sine):
    fine, coarse = rt.shape
    return pl.pallas_call(
        own_kernel,
        out_shape=(
            jax.ShapeDtypeStruct((coarse, coarse), F32),
            jax.ShapeDtypeStruct((coarse, coarse), F32),
        ),
        in_specs=[VMEM] * 8,
        out_specs=(VMEM, VMEM),
        scratch_shapes=[pltpu.VMEM((3, coarse, fine), BF16)],
        compiler_params=room(12),
        name="own_stage",
    )(src0, pot, near, far, side_faces, end, rt, sine)


def rows_kernel(own_ref, near_ref, sine_ref, far_ref, out_ref):
    devices, _, rows, coarse = out_ref.shape
    first = dot6(sine_ref, own_ref[...] + near_ref[...])
    out_ref[:, 0] = first.reshape(devices, rows, coarse)
    out_ref[:, 1] = far_ref[...].reshape(devices, rows, coarse)


def row_transform(coarse, devices):
    return split_matrix(sine_matrix(coarse)[mode_order(coarse, devices)], 3)


def rows_stage(devices, own, near, far, sine):
    coarse = own.shape[0]
    shape = (devices, 2, coarse // devices, coarse)
    return pl.pallas_call(
        rows_kernel,
        out_shape=jax.ShapeDtypeStruct(shape, F32),
        in_specs=[VMEM] * 4,
        out_specs=VMEM,
        compiler_params=room(8),
        name="rows_stage",
    )(own, near, sine, far)


def sweep_kernel(in_ref, alpha_ref, out_ref, values, force):
    planes, _, rows, coarse = in_ref.shape
    paired = rows % 2 == 0
    sixth = 1.0 / 6.0
    shape = (rows, LANES)
    count = coarse // LANES
    lanes = lax.broadcasted_iota(jnp.int32, shape, 1)
    alpha = jnp.broadcast_to(alpha_ref[place()[0]][:, 0:1], shape)
    zero = [jnp.zeros(shape, F32)] * count
    columns = [pl.ds(c * LANES, LANES) for c in range(count)]
    for k in range(planes):
        total = in_ref[k, 0]
        if k % 2 == 0 and k > 0:
            total = total + in_ref[k - 1, 1]
        if k % 2 == 1 and k + 1 < planes:
            total = total + in_ref[k + 1, 1]
        total = total * sixth
        force[k] = total
        values[k] = total

    def held(k):
        return [values[k, :, columns[c]] for c in range(count)]

    def applied(k, under, here, over):
        sums = beside_columns(here, lanes)
        return [
            (force[k, :, columns[c]] + alpha * here[c]) + sixth * ((under[c] + over[c]) + sums[c])
            for c in range(count)
        ]

    def step(counter, carry):
        under, here = zero, held(0)
        for k in range(planes):
            over = held(k + 1) if k + 1 < planes else zero
            for c, value in enumerate(applied(k, under, here, over)):
                values[k, :, columns[c]] = value
            under, here = here, over
        return carry

    lax.fori_loop(0, 2 * SWEEPS - 2, step, 0)

    under, here = zero, held(0)
    for k in range(planes):
        over = held(k + 1) if k + 1 < planes else zero
        black = applied(k, under, here, over)
        for c in range(count):
            mean = 0.5 * (here[c] + black[c])
            swing = 0.5 * (here[c] - black[c])
            swing = swing * column_sign(lanes, count, k, c)
            fields = [mean + pltpu.roll(swing, rows // 2, 0)] if paired else [mean, swing]
            for f, field in enumerate(fields):
                store_solved(out_ref, planes, k, c, f * rows, field)
        under, here = here, over


def packed_sweep_kernel(in_ref, alpha_ref, out_ref, red, black, red_force, black_force):
    planes, _, rows, coarse = in_ref.shape
    slots = planes // 2
    half = rows // 2
    sixth = 1.0 / 6.0
    shape = (rows, LANES)
    count = coarse // LANES
    lanes = lax.broadcasted_iota(jnp.int32, shape, 1)
    first = lax.broadcasted_iota(jnp.int32, shape, 0) < half
    alpha = alpha_ref[place()[0]]
    zero = jnp.zeros(shape, F32)
    columns = [pl.ds(c * LANES, LANES) for c in range(count)]
    signs = [[column_sign(lanes, count, q, c) for c in range(count)] for q in (0, 1)]

    def forcing(k, c):
        total = in_ref[k, 0, :, columns[c]]
        if k % 2 == 0 and k > 0:
            total = total + in_ref[k - 1, 1, :, columns[c]]
        if k % 2 == 1 and k + 1 < planes:
            total = total + in_ref[k + 1, 1, :, columns[c]]
        return total

    def swapped(x):
        return pltpu.roll(x, half, 0)

    for q in range(slots):
        for c in range(count):
            one, two = forcing(q, c), forcing(q + slots, c)
            low = jnp.where(first, one, swapped(two)) * (0.5 * sixth)
            high = jnp.where(first, swapped(one), two) * (0.5 * sixth * signs[q % 2][c])
            red_force[q, :, columns[c]] = low + high
            black_force[q, :, columns[c]] = low - high
            red[q, :, columns[c]] = low + high

    def update(target, force, other):
        def held(q):
            return [other[q, :, columns[c]] for c in range(count)]

        here, end = held(0), held(slots - 1)
        under = [jnp.where(first, zero, swapped(x)) for x in end]
        beyond = [jnp.where(first, swapped(x), zero) for x in here]
        for q in range(slots):
            over = held(q + 1) if q + 1 < slots else beyond
            sums = beside_columns(here, lanes)
            for c in range(count):
                target[q, :, columns[c]] = (force[q, :, columns[c]] + alpha * here[c]) + sixth * (
                    (under[c] + over[c]) + sums[c]
                )
            under, here = here, over

    update(black, black_force, red)

    def sweep(counter, carry):
        update(red, red_force, black)
        update(black, black_force, red)
        return carry

    lax.fori_loop(0, SWEEPS - 1, sweep, 0, unroll=True)

    for q in range(slots):
        for c in range(count):
            on_red, on_black = red[q, :, columns[c]], black[q, :, columns[c]]
            low = on_red + on_black
            high = signs[q % 2][c] * (on_red - on_black)
            store_solved(out_ref, planes, q, c, 0, jnp.where(first, low, swapped(high)))
            store_solved(out_ref, planes, q + slots, c, 0, jnp.where(first, swapped(low), high))


def store_solved(out_ref, planes, k, c, first_row, field):
    rows = field.shape[0]
    coarse = out_ref.shape[2] // 3 * 2
    where = pl.ds(first_row, rows)
    out_ref[k, where, pl.ds(c * LANES, LANES)] = field
    if k >= 2 and k % 2 == 0 or k == planes - 1:
        half = coarse // 2
        before = k - 2 if k < planes - 1 else k - 1
        side = c * LANES // half
        out_ref[before + side, where, pl.ds(coarse + c * LANES - side * half, LANES)] = field


def sweep_stage(received):
    devices, _, rows, coarse = received.shape
    packed = rows == 8 and devices % 4 == 0
    fields = 1 if rows % 2 == 0 else 2
    modes = (mode_order(coarse, devices) + 1).reshape(devices, rows)
    if packed:
        modes = np.concatenate([modes[:, : rows // 2]] * 2, 1)
    alpha = np.cos(np.pi * modes / (coarse + 1)) / 3.0
    table = jnp.asarray(np.tile(alpha[:, :, None], (1, 1, LANES)), F32)
    shape = (devices // 2 if packed else devices, rows, coarse)
    return pl.pallas_call(
        packed_sweep_kernel if packed else sweep_kernel,
        out_shape=jax.ShapeDtypeStruct((devices, fields * rows, coarse + coarse // 2), F32),
        in_specs=[VMEM, VMEM],
        out_specs=VMEM,
        scratch_shapes=[pltpu.VMEM(shape, F32)] * (4 if packed else 2),
        compiler_params=room(8 if rows % 8 == 0 else 24),
        name="sweep_stage",
    )(received, table)


def back_product(in_ref, back_ref, first, size):
    devices, held, _ = in_ref.shape
    coarse = back_ref.shape[1]
    rows = coarse // devices
    total = None
    for f in range(held // rows):
        part = in_ref[:, f * rows : (f + 1) * rows, first : first + size].reshape(coarse, size)
        term = dot6(back_ref.at[pl.ds(3 * f, 3)], part)
        total = term if total is None else total + term
    return total


def by_parity(even, odd):
    is_even = lax.rem(place()[0], 2) == 0
    pl.when(is_even)(even)
    pl.when(jnp.logical_not(is_even))(odd)


def swap_kernel(in_ref, back_ref, swap_ref):
    coarse = swap_ref.shape[0]
    half = in_ref.shape[2] - coarse

    def even():
        swap_ref[:, 0:half] = back_product(in_ref, back_ref, coarse, half)
        swap_ref[:, half:] = jnp.zeros((coarse, coarse - half), F32)

    def odd():
        swap_ref[...] = back_product(in_ref, back_ref, 0, coarse)

    by_parity(even, odd)


def back_matrices(coarse, devices, held):
    order = mode_order(coarse, devices)
    sine = sine_matrix(coarse)
    back = [sine[order].T]
    if held > coarse // devices:
        back.append(sine[coarse - 1 - order].T)
    return jnp.concatenate([split_matrix(matrix, 3) for matrix in back])


def swap_stage(coarse, received, back):
    return pl.pallas_call(
        swap_kernel,
        out_shape=jax.ShapeDtypeStruct((coarse, coarse), F32),
        in_specs=[VMEM, VMEM],
        out_specs=VMEM,
        compiler_params=room(16),
        name="swap_stage",
    )(received, back)


def add_prolonged(value, pt_ref, pot, plane, out, parts, wide, ready):
    coarse = value.shape[0]
    fine = 2 * coarse
    block = 64
    for part, piece in enumerate(split3(value)):
        parts[part] = piece
    for n in range(0, fine, coarse):
        wide[0:coarse, :] = dot3(parts, 0, pt_ref[:, n : n + coarse])
        wide[coarse : coarse + 1, :] = wide[coarse - 1 : coarse, :]
        for c in range(n // LANES, (n + coarse) // LANES):
            lanes = pl.ds(c * LANES - n, LANES)
            for start in range(0, coarse, block):
                here = wide[pl.ds(start, block), lanes]
                after = wide[pl.ds(start + 1, block), lanes]
                for odd, value in ((0, here), (1, 0.5 * (here + after))):
                    old = pot[plane, c, pl.ds(PAD + 2 * start + odd, block, stride=2), :]
                    out[c, pl.ds(2 * start + odd, block, stride=2), :] = old + value
            ready(c)


def even_kernel(in_ref, back_ref, swap_ref, pt_ref, pot, own_ref, extra_ref, out_ref, corr_ref, parts, wide):
    coarse, half = extra_ref.shape

    def even():
        own_ref[...] = back_product(in_ref, back_ref, 0, coarse)
        extra_ref[...] = swap_ref[:, 0:half]

    def odd():
        own_ref[...] = swap_ref[...]
        extra_ref[...] = back_product(in_ref, back_ref, coarse, half)

    by_parity(even, odd)
    add_prolonged(own_ref[...], pt_ref, pot, 0, out_ref, parts, wide, lambda c: None)
    corr_ref[...] = dot3(parts, 0, ordering(coarse, True))


def odd_kernel(
    own_ref, swapped_ref, extra_ref, even_ref, corr_ref, pt_ref, pot, out_hbm, corr_hbm, out, parts, wide, sem, corr_sem
):
    stores = [
        [
            pltpu.make_async_copy(
                buf.at[c], out_hbm.at[plane, :, pl.ds(c * LANES, LANES)], sem.at[plane * out.shape[0] + c]
            )
            for c in range(out.shape[0])
        ]
        for plane, buf in ((0, even_ref), (1, out))
    ]
    for store in stores[0]:
        store.start()
    copy = pltpu.make_async_copy(corr_ref, corr_hbm.at[0], corr_sem)
    copy.start()
    position, devices = place()
    own = own_ref[...]
    swapped = swapped_ref[...]
    half = extra_ref.shape[1]
    is_even = lax.rem(position, 2) == 0
    right = jnp.where(is_even, swapped[:, half:], extra_ref[...])
    above = jnp.concatenate([swapped[:, :half], right], 1)
    above = jnp.where(position == devices - 1, own, above)
    add_prolonged(
        0.5 * (own + above), pt_ref, pot, 1, out, parts, wide, lambda c: stores[1][c].start()
    )
    for store in stores[0] + stores[1]:
        store.wait()
    copy.wait()


def prolong_matrix(coarse):
    return jnp.asarray(prolongation(coarse).T[column_order(coarse)], BF16)


def plane_scratch(coarse):
    return [pltpu.VMEM((3, coarse, coarse), BF16), pltpu.VMEM((coarse + PAD, coarse), F32)]


def even_stage(received, back, swap, pot):
    coarse = swap.shape[0]
    fine = 2 * coarse
    return pl.pallas_call(
        even_kernel,
        out_shape=(
            jax.ShapeDtypeStruct((coarse, coarse), F32),
            jax.ShapeDtypeStruct((coarse, received.shape[2] - coarse), F32),
            jax.ShapeDtypeStruct((fine // LANES, fine, LANES), F32),
            jax.ShapeDtypeStruct((coarse, coarse), F32),
        ),
        in_specs=[VMEM] * 5,
        out_specs=(VMEM,) * 4,
        scratch_shapes=plane_scratch(coarse),
        compiler_params=room(16),
        name="even_stage",
    )(received, back, swap, prolong_matrix(coarse), pot)


def odd_stage(own, swapped, extra, even, corr, pot):
    coarse = own.shape[0]
    fine = 2 * coarse
    blocks = fine // LANES
    return pl.pallas_call(
        odd_kernel,
        out_shape=(
            jax.ShapeDtypeStruct((2, fine, fine), F32),
            jax.ShapeDtypeStruct((1, coarse, coarse), F32),
        ),
        in_specs=[VMEM] * 7,
        out_specs=(HBM, HBM),
        scratch_shapes=[pltpu.VMEM((blocks, fine, LANES), F32)]
        + plane_scratch(coarse)
        + [pltpu.SemaphoreType.DMA((2 * blocks,)), pltpu.SemaphoreType.DMA],
        compiler_params=room(8),
        name="odd_stage",
    )(own, swapped, extra, even, corr, prolong_matrix(coarse), pot)


def per_device(potential, source, side_faces, end_faces):
    devices = lax.axis_size("grp") * lax.axis_size("mem")
    coarse = side_faces.shape[2]
    in_chip = [(i, i ^ 1) for i in range(devices)]
    near, far, pot, src0, end, rt, sine = sent_stage(devices, potential, source, end_faces)
    arrived = lax.ppermute(near, AXES, in_chip)
    own, far = own_stage(src0, pot, near, far, side_faces, end, rt, sine)
    sent = rows_stage(devices, own, arrived, far, sine)
    received = lax.all_to_all(sent, AXES, 0, 0, tiled=True)
    solved = sweep_stage(received)
    returned = lax.all_to_all(solved, AXES, 0, 0, tiled=True)
    back = back_matrices(coarse, devices, returned.shape[1])
    swap = swap_stage(coarse, returned, back)
    swapped = lax.ppermute(swap, AXES, in_chip)
    own, extra, even, corr = even_stage(returned, back, swap, pot)
    return odd_stage(own, swapped, extra, even, corr, pot)


def solution(mesh):
    split = P(AXES, None, None)
    return jax.shard_map(
        per_device,
        mesh=mesh,
        in_specs=(split, split, split, P()),
        out_specs=(split, split),
        check_vma=False,
    )
```

```python
import jax
import jax.numpy as jnp
import numpy as np
from jax import lax
from jax.experimental import pallas as pl
from jax.experimental.pallas import tpu as pltpu
from jax.sharding import PartitionSpec as P

SWEEPS = 8
AXES = ("grp", "mem")
PAD = 8
LANES = 128
F32 = jnp.float32
BF16 = jnp.bfloat16
VMEM = pl.BlockSpec(memory_space=pltpu.VMEM)
ANY = pl.BlockSpec(memory_space=pl.ANY)
HBM = pl.BlockSpec(memory_space=pltpu.HBM)


def place():
    members = lax.axis_size("mem")
    return lax.axis_index("grp") * members + lax.axis_index("mem"), lax.axis_size("grp") * members


def in_hbm(array):
    return pltpu.with_memory_space_constraint(array, pltpu.HBM)


def room(mebibytes):
    return pltpu.CompilerParams(vmem_limit_bytes=mebibytes << 20)


def restriction(fine):
    matrix = np.zeros((fine // 2, fine))
    for i in range(fine // 2):
        matrix[i, 2 * i] = 0.5
        matrix[i, 2 * i + 1] = 0.25
        if i > 0:
            matrix[i, 2 * i - 1] = 0.25
    return matrix


def neighbour_sum(n):
    return np.eye(n, k=1) + np.eye(n, k=-1)


def prolongation(coarse):
    matrix = np.zeros((2 * coarse, coarse))
    for i in range(coarse):
        matrix[2 * i, i] = 1.0
        matrix[2 * i + 1, i] += 0.5
        matrix[2 * i + 1, min(i + 1, coarse - 1)] += 0.5
    return matrix


def column_order(coarse):
    columns = np.arange(coarse)
    return np.concatenate([columns[0::2], columns[1::2]]) if coarse == 2 * LANES else columns


def ordering(coarse, back):
    held = lax.broadcasted_iota(jnp.int32, (coarse, coarse), 0 if back else 1)
    natural = lax.broadcasted_iota(jnp.int32, (coarse, coarse), 1 if back else 0)
    if coarse == 2 * LANES:
        held = jnp.where(held < LANES, 2 * held, 2 * (held - LANES) + 1)
    return jnp.where(held == natural, 1.0, 0.0).astype(BF16)


def dot_exact(x, weights):
    total = None
    for part in reversed(split3(x)):
        term = jnp.dot(part, weights, preferred_element_type=F32)
        total = term if total is None else total + term
    return total


def mode_order(n, devices):
    rows = n // devices
    if rows % 2:
        return np.arange(n)
    half = rows // 2
    low = np.arange(n // 2).reshape(devices, half)
    return np.concatenate([low, n - 1 - low], 1).reshape(-1)


def sine_matrix(n):
    index = np.arange(1, n + 1)
    return np.sqrt(2.0 / (n + 1)) * np.sin(np.pi * np.outer(index, index) / (n + 1))


def split3(x):
    high = x.astype(BF16)
    rest = x - high.astype(F32)
    mid = rest.astype(BF16)
    low = (rest - mid.astype(F32)).astype(BF16)
    return high, mid, low


def split_matrix(matrix, count):
    parts, rest = [], np.asarray(matrix, np.float64)
    for _ in range(count):
        parts.append(rest.astype(jnp.bfloat16))
        rest = rest - parts[-1].astype(np.float64)
    return jnp.asarray(np.stack(parts))


def dot6(matrix_ref, x):
    x = split3(x)
    total = None
    for left, right in ((2, 0), (0, 2), (1, 1), (1, 0), (0, 1), (0, 0)):
        term = jnp.dot(matrix_ref[left], x[right], preferred_element_type=F32)
        total = term if total is None else total + term
    return total


def dot3(parts_ref, first, weights):
    total = None
    for part in (2, 1, 0):
        term = jnp.dot(parts_ref[first + part], weights, preferred_element_type=F32)
        total = term if total is None else total + term
    return total


def restricted_rows(buf, index, start, block):
    def rows(offset):
        return buf[index + (pl.ds(PAD + 2 * start + offset, block, stride=2), slice(None))]

    return rows


def beside(parts, lanes):
    count = len(parts)
    after = [pltpu.roll(part, 1, 1) for part in parts]
    before = [pltpu.roll(part, LANES - 1, 1) for part in parts]
    sums = []
    for c in range(count):
        left = jnp.where(lanes == 0, after[c - 1] if c > 0 else 0.0, after[c])
        right = jnp.where(lanes == LANES - 1, before[c + 1] if c + 1 < count else 0.0, before[c])
        sums.append(left + right)
    return sums


def around(rows, even, row_ids, start):
    outer = rows(-2) + rows(2)
    if start == 0:
        outer = outer - jnp.where(row_ids == 0, even, 0.0)
    return outer - (even + even)


def in_plane(quad, outer, lanes):
    sums = beside(quad, lanes)
    return [(outer[c] + sums[c]) - 4.0 * quad[c] for c in range(len(quad))]


def beside_columns(parts, lanes):
    if len(parts) != 2:
        return beside(parts, lanes)
    even, odd = parts
    return [
        odd + jnp.where(lanes == 0, 0.0, pltpu.roll(odd, 1, 1)),
        even + jnp.where(lanes == LANES - 1, 0.0, pltpu.roll(even, LANES - 1, 1)),
    ]


def column_sign(lanes, count, k, c):
    if count == 2:
        return jnp.full(lanes.shape, 1.0 if (k + c) % 2 == 0 else -1.0, F32)
    return jnp.where((lanes + k) % 2 == 0, 1.0, -1.0)


def sent_kernel(
    pot_hbm, src_hbm, end_hbm, sine_hbm,
    near_ref, far_ref, pot, src0, end, rt_ref, sine_ref,
    src, mid, parts, sem, small_sem,
):
    fine = pot_hbm.shape[1]
    coarse = fine // 2
    blocks = fine // LANES
    cut = fine // 2 + 2 * PAD
    position, devices = place()
    groups = []
    for hbm, plane, buf, index in (
        (pot_hbm, 0, pot, (0,)), (pot_hbm, 1, pot, (1,)), (src_hbm, 1, src, ()), (src_hbm, 0, src0, ()),
    ):
        for first, size in ((0, fine),):
            group = []
            for c in range(blocks):
                group.append(
                    pltpu.make_async_copy(
                        hbm.at[plane, pl.ds(first, size), pl.ds(c * LANES, LANES)],
                        buf.at[index + (c, pl.ds(PAD + first, size), slice(None))],
                        sem.at[len(groups) * blocks + c],
                    )
                )
            groups.append(group)
    for group in groups[:1]:
        for copy in group:
            copy.start()
    for group in groups[1:3]:
        for copy in group:
            copy.start()
    for copy in groups[3]:
        copy.start(priority=1)
    sine = pltpu.make_async_copy(sine_hbm, sine_ref, small_sem.at[1])
    sine.start(priority=1)
    last = devices - 1
    at_end = jnp.logical_or(position == 0, position == last)
    end_copy = pltpu.make_async_copy(end_hbm.at[jnp.where(position == last, 1, 0)], end, small_sem.at[2])

    @pl.when(at_end)
    def _():
        end_copy.start()

    target = lax.broadcasted_iota(jnp.int32, rt_ref.shape, 1)
    if coarse == 2 * LANES:
        target = jnp.where(target < LANES, 2 * target, 2 * (target - LANES) + 1)
    offset = lax.broadcasted_iota(jnp.int32, rt_ref.shape, 0) - 2 * target
    beside_even = jnp.where(jnp.abs(offset) == 1, 0.25, 0.0)
    rt_ref[...] = jnp.where(offset == 0, 0.5, beside_even).astype(BF16)
    edge = jnp.zeros((blocks, PAD, LANES), F32)
    for ref in (pot.at[0], pot.at[1], src, src0):
        ref[:, 0:PAD, :] = edge
        ref[:, PAD + fine : PAD + fine + PAD, :] = edge

    block = 32
    lanes = lax.broadcasted_iota(jnp.int32, (block, LANES), 1)
    row_ids = lax.broadcasted_iota(jnp.int32, (block, LANES), 0)

    def chunk(plane, start):
        where = pl.ds(start, block)
        quad, whole = [], []
        for c in range(blocks):
            rows = restricted_rows(pot, (plane, c), start, block)
            even = rows(0)
            quad.append((even + even) + (rows(1) + rows(-1)))
            if plane == 1:
                whole.append(around(rows, even, row_ids, start))
        if plane == 1:
            whole = in_plane(quad, whole, lanes)
        for c in range(blocks):
            columns = pl.ds(c * LANES, LANES)
            if plane == 0:
                mid[where, columns] = quad[c]
                pieces(0, where, columns, quad[c])
            else:
                rows = restricted_rows(src, (c,), start, block)
                even = rows(0)
                source = (even + even) + (rows(1) + rows(-1))
                value = (whole[c] + 0.25 * source) + ((quad[c] + quad[c]) + mid[where, columns])
                pieces(3, where, columns, value)

    def pieces(first, where, columns, value):
        for part, piece in enumerate(split3(value)):
            parts[first + part, where, columns] = piece

    starts = range(0, coarse, block)
    for copy in groups[0]:
        copy.wait()
    for start in starts:
        chunk(0, start)
    for group in groups[1:3]:
        for copy in group:
            copy.wait()
    for start in starts:
        chunk(1, start)
    down = 0.25 * dot3(parts, 0, rt_ref[...])
    up = 0.25 * dot3(parts, 3, rt_ref[...])
    is_even = lax.rem(position, 2) == 0
    near_ref[...] = jnp.where(is_even, up, down)
    far_ref[...] = jnp.where(is_even, down, up)
    for group in groups[3:]:
        for copy in group:
            copy.wait()
    sine.wait()

    @pl.when(at_end)
    def _():
        end_copy.wait()


def restriction_matrix(fine):
    return jnp.asarray(restriction(fine).T, BF16)


def sent_stage(devices, potential, source, end_faces):
    fine = potential.shape[1]
    coarse = fine // 2
    blocks = fine // LANES
    plane = jax.ShapeDtypeStruct((coarse, coarse), F32)
    held = (blocks, fine + 2 * PAD, LANES)
    return pl.pallas_call(
        sent_kernel,
        out_shape=(
            plane,
            plane,
            jax.ShapeDtypeStruct((2,) + held, F32),
            jax.ShapeDtypeStruct(held, F32),
            plane,
            jax.ShapeDtypeStruct((fine, coarse), BF16),
            jax.ShapeDtypeStruct((3, coarse, coarse), BF16),
        ),
        in_specs=[HBM] * 4,
        out_specs=(VMEM,) * 7,
        scratch_shapes=[
            pltpu.VMEM(held, F32),
            pltpu.VMEM((coarse, fine), F32),
            pltpu.VMEM((6, coarse, fine), BF16),
            pltpu.SemaphoreType.DMA((8 * blocks,)),
            pltpu.SemaphoreType.DMA((3,)),
        ],
        compiler_params=room(20),
        name="sent_stage",
    )(
        in_hbm(potential), in_hbm(source), in_hbm(end_faces),
        in_hbm(row_transform(coarse, devices)),
    )


def own_kernel(src0, pot, near_ref, far_ref, side_ref, end, rt_ref, sine_ref, own_ref, sent_ref, parts):
    fine, coarse = rt_ref.shape
    position, devices = place()
    last = devices - 1
    half_not_first = jnp.where(position > 0, 0.5, 0.0).astype(F32)
    block = 32
    shape = (block, LANES)
    lanes = lax.broadcasted_iota(jnp.int32, shape, 1)
    row_ids = lax.broadcasted_iota(jnp.int32, shape, 0)
    for start in range(0, coarse, block):
        where = pl.ds(start, block)
        quad, outer = [], []
        for c in range(fine // LANES):
            rows = restricted_rows(pot, (0, c), start, block)
            even = rows(0)
            quad.append((even + even) + (rows(1) + rows(-1)))
            outer.append(around(rows, even, row_ids, start))
        whole = in_plane(quad, outer, lanes)
        for c in range(fine // LANES):
            rows = restricted_rows(src0, (c,), start, block)
            even = rows(0)
            source = (even + even) + (rows(1) + rows(-1))
            value = (whole[c] + half_not_first * quad[c]) + 0.25 * source
            for part, piece in enumerate(split3(value)):
                parts[part, where, pl.ds(c * LANES, LANES)] = piece
    sent_ref[...] = dot6(sine_ref, far_ref[...])
    up = jnp.where(lax.rem(position, 2) == 0, near_ref[...], far_ref[...])
    own_ref[...] = 0.5 * dot3(parts, 0, rt_ref[...]) + up
    side = side_ref[0]
    columns = jnp.transpose(jnp.concatenate([side, side], 0))
    order = ordering(coarse, False)
    ends = dot_exact(jnp.concatenate([side, side], 0), order)
    own_ref[0:1, :] += ends[0:1]
    own_ref[coarse - 1 : coarse, :] += ends[1:2]
    lanes = lax.broadcasted_iota(jnp.int32, (coarse, LANES), 1)
    own_ref[:, 0:LANES] += jnp.where(lanes == 0, columns[:, 2:3], 0.0)
    own_ref[:, coarse - LANES : coarse] += jnp.where(lanes == LANES - 1, columns[:, 3:4], 0.0)

    @pl.when(jnp.logical_or(position == 0, position == last))
    def _():
        own_ref[...] += dot_exact(end[...], order)


def own_stage(src0, pot, near, far, side_faces, end, rt, sine):
    fine, coarse = rt.shape
    return pl.pallas_call(
        own_kernel,
        out_shape=(
            jax.ShapeDtypeStruct((coarse, coarse), F32),
            jax.ShapeDtypeStruct((coarse, coarse), F32),
        ),
        in_specs=[VMEM] * 8,
        out_specs=(VMEM, VMEM),
        scratch_shapes=[pltpu.VMEM((3, coarse, fine), BF16)],
        compiler_params=room(12),
        name="own_stage",
    )(src0, pot, near, far, side_faces, end, rt, sine)


def rows_kernel(own_ref, near_ref, sine_ref, far_ref, out_ref):
    devices, _, rows, coarse = out_ref.shape
    first = dot6(sine_ref, own_ref[...] + near_ref[...])
    out_ref[:, 0] = first.reshape(devices, rows, coarse)
    out_ref[:, 1] = far_ref[...].reshape(devices, rows, coarse)


def row_transform(coarse, devices):
    return split_matrix(sine_matrix(coarse)[mode_order(coarse, devices)], 3)


def rows_stage(devices, own, near, far, sine):
    coarse = own.shape[0]
    shape = (devices, 2, coarse // devices, coarse)
    return pl.pallas_call(
        rows_kernel,
        out_shape=jax.ShapeDtypeStruct(shape, F32),
        in_specs=[VMEM] * 4,
        out_specs=VMEM,
        compiler_params=room(8),
        name="rows_stage",
    )(own, near, sine, far)


def sweep_kernel(in_ref, alpha_ref, out_ref, values, force):
    planes, _, rows, coarse = in_ref.shape
    paired = rows % 2 == 0
    sixth = 1.0 / 6.0
    shape = (rows, LANES)
    count = coarse // LANES
    lanes = lax.broadcasted_iota(jnp.int32, shape, 1)
    alpha = jnp.broadcast_to(alpha_ref[place()[0]][:, 0:1], shape)
    zero = [jnp.zeros(shape, F32)] * count
    columns = [pl.ds(c * LANES, LANES) for c in range(count)]
    for k in range(planes):
        total = in_ref[k, 0]
        if k % 2 == 0 and k > 0:
            total = total + in_ref[k - 1, 1]
        if k % 2 == 1 and k + 1 < planes:
            total = total + in_ref[k + 1, 1]
        total = total * sixth
        force[k] = total
        values[k] = total

    def held(k):
        return [values[k, :, columns[c]] for c in range(count)]

    def applied(k, under, here, over):
        sums = beside_columns(here, lanes)
        return [
            (force[k, :, columns[c]] + alpha * here[c]) + sixth * ((under[c] + over[c]) + sums[c])
            for c in range(count)
        ]

    def step(counter, carry):
        under, here = zero, held(0)
        for k in range(planes):
            over = held(k + 1) if k + 1 < planes else zero
            for c, value in enumerate(applied(k, under, here, over)):
                values[k, :, columns[c]] = value
            under, here = here, over
        return carry

    lax.fori_loop(0, 2 * SWEEPS - 2, step, 0)

    under, here = zero, held(0)
    for k in range(planes):
        over = held(k + 1) if k + 1 < planes else zero
        black = applied(k, under, here, over)
        for c in range(count):
            mean = 0.5 * (here[c] + black[c])
            swing = 0.5 * (here[c] - black[c])
            swing = swing * column_sign(lanes, count, k, c)
            fields = [mean + pltpu.roll(swing, rows // 2, 0)] if paired else [mean, swing]
            for f, field in enumerate(fields):
                store_solved(out_ref, planes, k, c, f * rows, field)
        under, here = here, over


def packed_sweep_kernel(in_ref, alpha_ref, out_ref, red, black, red_force, black_force):
    planes, _, rows, coarse = in_ref.shape
    slots = planes // 2
    half = rows // 2
    sixth = 1.0 / 6.0
    shape = (rows, LANES)
    count = coarse // LANES
    lanes = lax.broadcasted_iota(jnp.int32, shape, 1)
    first = lax.broadcasted_iota(jnp.int32, shape, 0) < half
    alpha = alpha_ref[place()[0]]
    zero = jnp.zeros(shape, F32)
    columns = [pl.ds(c * LANES, LANES) for c in range(count)]
    signs = [[column_sign(lanes, count, q, c) for c in range(count)] for q in (0, 1)]

    def forcing(k, c):
        total = in_ref[k, 0, :, columns[c]]
        if k % 2 == 0 and k > 0:
            total = total + in_ref[k - 1, 1, :, columns[c]]
        if k % 2 == 1 and k + 1 < planes:
            total = total + in_ref[k + 1, 1, :, columns[c]]
        return total

    def swapped(x):
        return pltpu.roll(x, half, 0)

    for q in range(slots):
        for c in range(count):
            one, two = forcing(q, c), forcing(q + slots, c)
            low = jnp.where(first, one, swapped(two)) * (0.5 * sixth)
            high = jnp.where(first, swapped(one), two) * (0.5 * sixth * signs[q % 2][c])
            red_force[q, :, columns[c]] = low + high
            black_force[q, :, columns[c]] = 6.0 * (low - high)
            red[q, :, columns[c]] = low + high

    def update(target, force, other, centre, scale):
        def held(q):
            return [other[q, :, columns[c]] for c in range(count)]

        here, end = held(0), held(slots - 1)
        under = [jnp.where(first, zero, swapped(x)) for x in end]
        beyond = [jnp.where(first, swapped(x), zero) for x in here]
        for q in range(slots):
            over = held(q + 1) if q + 1 < slots else beyond
            sums = beside_columns(here, lanes)
            for c in range(count):
                around_it = (under[c] + over[c]) + sums[c]
                if scale is not None:
                    around_it = scale * around_it
                target[q, :, columns[c]] = (force[q, :, columns[c]] + centre * here[c]) + around_it
            under, here = here, over

    update(black, black_force, red, 6.0 * alpha, None)

    def sweep(counter, carry):
        update(red, red_force, black, sixth * alpha, sixth * sixth)
        update(black, black_force, red, 6.0 * alpha, None)
        return carry

    lax.fori_loop(0, SWEEPS - 1, sweep, 0, unroll=True)

    for q in range(slots):
        for c in range(count):
            on_red, on_black = red[q, :, columns[c]], sixth * black[q, :, columns[c]]
            low = on_red + on_black
            high = signs[q % 2][c] * (on_red - on_black)
            store_solved(out_ref, planes, q, c, 0, jnp.where(first, low, swapped(high)))
            store_solved(out_ref, planes, q + slots, c, 0, jnp.where(first, swapped(low), high))


def store_solved(out_ref, planes, k, c, first_row, field):
    rows = field.shape[0]
    coarse = out_ref.shape[2] // 3 * 2
    where = pl.ds(first_row, rows)
    out_ref[k, where, pl.ds(c * LANES, LANES)] = field
    if k >= 2 and k % 2 == 0 or k == planes - 1:
        half = coarse // 2
        before = k - 2 if k < planes - 1 else k - 1
        side = c * LANES // half
        out_ref[before + side, where, pl.ds(coarse + c * LANES - side * half, LANES)] = field


def sweep_stage(received):
    devices, _, rows, coarse = received.shape
    packed = rows == 8 and devices % 4 == 0
    fields = 1 if rows % 2 == 0 else 2
    modes = (mode_order(coarse, devices) + 1).reshape(devices, rows)
    if packed:
        modes = np.concatenate([modes[:, : rows // 2]] * 2, 1)
    alpha = np.cos(np.pi * modes / (coarse + 1)) / 3.0
    table = jnp.asarray(np.tile(alpha[:, :, None], (1, 1, LANES)), F32)
    shape = (devices // 2 if packed else devices, rows, coarse)
    return pl.pallas_call(
        packed_sweep_kernel if packed else sweep_kernel,
        out_shape=jax.ShapeDtypeStruct((devices, fields * rows, coarse + coarse // 2), F32),
        in_specs=[VMEM, VMEM],
        out_specs=VMEM,
        scratch_shapes=[pltpu.VMEM(shape, F32)] * (4 if packed else 2),
        compiler_params=room(8 if rows % 8 == 0 else 24),
        name="sweep_stage",
    )(received, table)


def back_product(in_ref, back_ref, first, size):
    devices, held, _ = in_ref.shape
    coarse = back_ref.shape[1]
    rows = coarse // devices
    total = None
    for f in range(held // rows):
        part = in_ref[:, f * rows : (f + 1) * rows, first : first + size].reshape(coarse, size)
        term = dot6(back_ref.at[pl.ds(3 * f, 3)], part)
        total = term if total is None else total + term
    return total


def by_parity(even, odd):
    is_even = lax.rem(place()[0], 2) == 0
    pl.when(is_even)(even)
    pl.when(jnp.logical_not(is_even))(odd)


def swap_kernel(in_ref, back_ref, swap_ref):
    coarse = swap_ref.shape[0]
    half = in_ref.shape[2] - coarse

    def even():
        swap_ref[:, 0:half] = back_product(in_ref, back_ref, coarse, half)
        swap_ref[:, half:] = jnp.zeros((coarse, coarse - half), F32)

    def odd():
        swap_ref[...] = back_product(in_ref, back_ref, 0, coarse)

    by_parity(even, odd)


def back_matrices(coarse, devices, held):
    order = mode_order(coarse, devices)
    sine = sine_matrix(coarse)
    back = [sine[order].T]
    if held > coarse // devices:
        back.append(sine[coarse - 1 - order].T)
    return jnp.concatenate([split_matrix(matrix, 3) for matrix in back])


def swap_stage(coarse, received, back):
    return pl.pallas_call(
        swap_kernel,
        out_shape=jax.ShapeDtypeStruct((coarse, coarse), F32),
        in_specs=[VMEM, VMEM],
        out_specs=VMEM,
        compiler_params=room(16),
        name="swap_stage",
    )(received, back)


def add_prolonged(value, pt_ref, pot, plane, out, parts, wide, ready):
    coarse = value.shape[0]
    fine = 2 * coarse
    block = 64
    for part, piece in enumerate(split3(value)):
        parts[part] = piece
    for n in range(0, fine, coarse):
        wide[0:coarse, :] = dot3(parts, 0, pt_ref[:, n : n + coarse])
        wide[coarse : coarse + 1, :] = wide[coarse - 1 : coarse, :]
        for c in range(n // LANES, (n + coarse) // LANES):
            lanes = pl.ds(c * LANES - n, LANES)
            for start in range(0, coarse, block):
                here = wide[pl.ds(start, block), lanes]
                after = wide[pl.ds(start + 1, block), lanes]
                for odd, value in ((0, here), (1, 0.5 * (here + after))):
                    old = pot[plane, c, pl.ds(PAD + 2 * start + odd, block, stride=2), :]
                    out[c, pl.ds(2 * start + odd, block, stride=2), :] = old + value
            ready(c)


def even_kernel(in_ref, back_ref, swap_ref, pt_ref, pot, own_ref, extra_ref, out_ref, corr_ref, parts, wide):
    coarse, half = extra_ref.shape

    def even():
        own_ref[...] = back_product(in_ref, back_ref, 0, coarse)
        extra_ref[...] = swap_ref[:, 0:half]

    def odd():
        own_ref[...] = swap_ref[...]
        extra_ref[...] = back_product(in_ref, back_ref, coarse, half)

    by_parity(even, odd)
    add_prolonged(own_ref[...], pt_ref, pot, 0, out_ref, parts, wide, lambda c: None)
    corr_ref[...] = dot3(parts, 0, ordering(coarse, True))


def odd_kernel(
    own_ref, swapped_ref, extra_ref, even_ref, corr_ref, pt_ref, pot, out_hbm, corr_hbm, out, parts, wide, sem, corr_sem
):
    stores = [
        [
            pltpu.make_async_copy(
                buf.at[c], out_hbm.at[plane, :, pl.ds(c * LANES, LANES)], sem.at[plane * out.shape[0] + c]
            )
            for c in range(out.shape[0])
        ]
        for plane, buf in ((0, even_ref), (1, out))
    ]
    for store in stores[0]:
        store.start()
    copy = pltpu.make_async_copy(corr_ref, corr_hbm.at[0], corr_sem)
    copy.start()
    position, devices = place()
    own = own_ref[...]
    swapped = swapped_ref[...]
    half = extra_ref.shape[1]
    is_even = lax.rem(position, 2) == 0
    right = jnp.where(is_even, swapped[:, half:], extra_ref[...])
    above = jnp.concatenate([swapped[:, :half], right], 1)
    above = jnp.where(position == devices - 1, own, above)
    add_prolonged(
        0.5 * (own + above), pt_ref, pot, 1, out, parts, wide, lambda c: stores[1][c].start()
    )
    for store in stores[0] + stores[1]:
        store.wait()
    copy.wait()


def prolong_matrix(coarse):
    return jnp.asarray(prolongation(coarse).T[column_order(coarse)], BF16)


def plane_scratch(coarse):
    return [pltpu.VMEM((3, coarse, coarse), BF16), pltpu.VMEM((coarse + PAD, coarse), F32)]


def even_stage(received, back, swap, pot):
    coarse = swap.shape[0]
    fine = 2 * coarse
    return pl.pallas_call(
        even_kernel,
        out_shape=(
            jax.ShapeDtypeStruct((coarse, coarse), F32),
            jax.ShapeDtypeStruct((coarse, received.shape[2] - coarse), F32),
            jax.ShapeDtypeStruct((fine // LANES, fine, LANES), F32),
            jax.ShapeDtypeStruct((coarse, coarse), F32),
        ),
        in_specs=[VMEM] * 5,
        out_specs=(VMEM,) * 4,
        scratch_shapes=plane_scratch(coarse),
        compiler_params=room(16),
        name="even_stage",
    )(received, back, swap, prolong_matrix(coarse), pot)


def odd_stage(own, swapped, extra, even, corr, pot):
    coarse = own.shape[0]
    fine = 2 * coarse
    blocks = fine // LANES
    return pl.pallas_call(
        odd_kernel,
        out_shape=(
            jax.ShapeDtypeStruct((2, fine, fine), F32),
            jax.ShapeDtypeStruct((1, coarse, coarse), F32),
        ),
        in_specs=[VMEM] * 7,
        out_specs=(HBM, HBM),
        scratch_shapes=[pltpu.VMEM((blocks, fine, LANES), F32)]
        + plane_scratch(coarse)
        + [pltpu.SemaphoreType.DMA((2 * blocks,)), pltpu.SemaphoreType.DMA],
        compiler_params=room(8),
        name="odd_stage",
    )(own, swapped, extra, even, corr, prolong_matrix(coarse), pot)


def per_device(potential, source, side_faces, end_faces):
    devices = lax.axis_size("grp") * lax.axis_size("mem")
    coarse = side_faces.shape[2]
    in_chip = [(i, i ^ 1) for i in range(devices)]
    near, far, pot, src0, end, rt, sine = sent_stage(devices, potential, source, end_faces)
    arrived = lax.ppermute(near, AXES, in_chip)
    own, far = own_stage(src0, pot, near, far, side_faces, end, rt, sine)
    sent = rows_stage(devices, own, arrived, far, sine)
    received = lax.all_to_all(sent, AXES, 0, 0, tiled=True)
    solved = sweep_stage(received)
    returned = lax.all_to_all(solved, AXES, 0, 0, tiled=True)
    back = back_matrices(coarse, devices, returned.shape[1])
    swap = swap_stage(coarse, returned, back)
    swapped = lax.ppermute(swap, AXES, in_chip)
    own, extra, even, corr = even_stage(returned, back, swap, pot)
    return odd_stage(own, swapped, extra, even, corr, pot)


def solution(mesh):
    split = P(AXES, None, None)
    return jax.shard_map(
        per_device,
        mesh=mesh,
        in_specs=(split, split, split, P()),
        out_specs=(split, split),
        check_vma=False,
    )
```
